512 devices in a mesh: src: 16 (over y, core), vocab: 32 (over x, z).
Axes of the slice: x: 4, y: 8, z: 8, core: 2. Of those that a mesh axis runs over, the one named last changes fastest.
Arguments:
- queries: bfloat16 [8192, 2048], P('vocab', 'src'), may hold values from -35 to 35
- enc_keys: bfloat16 [32, 256, 2048], P('vocab', None, 'src'), may hold values from -4 to 4
- enc_values: bfloat16 [32, 256, 2048], P('vocab', None, 'src'), may hold values from -48 to 48
- source_lengths: int32 [32], P('vocab'), may hold values from 1 to 256, 4096 in all
- out_proj: bfloat16 [2048, 2048], P('src'), may hold values from -0.125 to 0.125
- dec_state: bfloat16 [8192, 2048], P('vocab', 'src'), may hold values from -24 to 24
- norm_gain: float32 [2048], P('src'), may hold values from 0.25 to 1.75
- norm_bias: float32 [2048], P('src'), may hold values from -3 to 3
- head_weight: bfloat16 [2048, 258048], P('src', 'vocab'), may hold values from -2 to 2
- shortlist: int32 [8192, 8], P('vocab'), may hold values from 0 to 2015, all different within a row; in each aligned block of 256 rows (0 to 255, 256 to 511, ...) at most 2 rows name the same one
- target_slot: int32 [8192], P('vocab'), may hold values from 0 to 7
- target_offset: int32 [8192], P('vocab'), may hold values from 0 to 127
Outputs:
- row_loss: float32 [8192], P('vocab')
- grad_state: float32 [8192, 2048], P('vocab', 'src')
The draws below stay inside these ranges and needn't reach their ends.
Inputs may be any that keep to these rules, and one draw needn't show every extreme that they name: `shortlist`: each row lists 8 different blocks; the rows of one sentence list one block at most 2 times.
All inputs are finite; a program needn't handle non-finite values. No bound on the sum of `source_lengths` on one device may be relied on, other than what follows from the above.
Results may differ from the reference program's by a relative error of at most 0.0055.
Values may be sent and summed in bfloat16 or wider, within the bound.
No kernel may reach another device: no remote copies, remote signals or barrier semaphores. Data moves between devices by JAX's collectives and lax.ppermute only.
A program may use at most 64 MiB of HBM per device.

```python
import math
import jax
import jax.numpy as jnp
import numpy as np
from jax import lax

D = 2048
H = 16
HD = 128
BLK = 128
K_LIST = 8
ROWS_DEV = 256
SRC_LEN = 256
SEQS = 32
TGT_ROWS = 8192
VOCAB_BLOCKS = 2016
VOCAB = 258048
MOST = 2


def leading_keys(key):
    root_key = jax.random.fold_in(key, 17)
    first_key, rest_key = jax.random.split(root_key)
    front_rows = jnp.clip(jax.random.normal(first_key, (SEQS, 2, D), jnp.float32), -4.0, 4.0)
    return (front_rows, rest_key)


def draw_enc_keys(key, part):
    front_rows, rest_key = leading_keys(key)
    others = jnp.clip(jax.random.normal(rest_key, (SEQS, SRC_LEN - 2, D), jnp.float32), -4.0, 4.0)
    return jnp.concatenate([front_rows, others], axis=1).astype(jnp.bfloat16)


def draw_queries(key, part):
    root_key = jax.random.fold_in(key, 23)
    first_key = jax.random.fold_in(root_key, 0)
    values_field = jnp.clip(jax.random.normal(first_key, (TGT_ROWS, D), jnp.float32), -4.0, 4.0)
    return values_field.astype(jnp.bfloat16)


def draw_dec_state(key, part):
    root_key = jax.random.fold_in(key, 31)
    first_key, second_key, third_key = jax.random.split(root_key, 3)
    row_scales = jnp.exp(jax.random.uniform(first_key, (TGT_ROWS, 1), jnp.float32, -1.3863, 0.9163))
    placing = jnp.arange(D, dtype=jnp.float32) / D
    col_rough = jnp.exp(jax.random.uniform(second_key, (D,), jnp.float32, -0.5108, 0.47))
    col_scales = 3.0 ** (placing - 0.5) * col_rough
    noises = jnp.clip(jax.random.normal(third_key, (TGT_ROWS, D), jnp.float32), -3.0, 3.0)
    values_field = noises * row_scales * col_scales
    return jnp.clip(values_field, -24.0, 24.0).astype(jnp.bfloat16)


def draw_head_weight(key, part):
    root_key = jax.random.fold_in(key, 47)
    scaling = 3.0 / D ** 0.5
    weights = jnp.clip(jax.random.normal(root_key, (D, VOCAB), jnp.float32), -4.0, 4.0) * scaling
    return weights.astype(jnp.bfloat16)


def with_ends(values, own_key, smallest, high):
    place = [jax.random.randint(jax.random.fold_in(own_key, axis), (), 0, length) for axis, length in enumerate(values.shape)]
    main_axis = values.shape.index(max(values.shape))
    neighbour = place[:main_axis] + [(place[main_axis] + 1) % values.shape[main_axis]] + place[main_axis + 1:]
    return values.at[tuple(place)].set(smallest).at[tuple(neighbour)].set(high)


def block_scale(stream_key, extent, cuts, least, high):
    level, own = 1.0, jax.random.fold_in(stream_key, 6)
    for position, blocks in cuts:
        steps = jnp.exp(jax.random.uniform(jax.random.fold_in(own, position), (blocks,), jnp.float32, least / len(cuts), high / len(cuts)))
        level = level * jnp.repeat(steps, extent[position] // blocks).reshape([-1 if axis == position else 1 for axis in range(len(extent))])
    return level


def profile(count, total, reach, slope):
    portions = [(1 << 20) // math.isqrt(grade ** slope) + 1 for grade in range(2, count + 1)]
    rest, given = total - reach - (count - 1), [1] * (count - 1)
    while rest > 0:
        free = [i for i in range(count - 1) if given[i] < reach]
        mass, left = sum([portions[i] for i in free]), rest
        for i in free:
            addition = min(reach - given[i], max(1, left * portions[i] // mass), rest)
            given[i] = given[i] + addition
            rest = rest - addition
    return np.array([reach] + given)


def uneven(own_key, amount, total, bound, lean):
    if amount == 2:
        one = jax.random.randint(own_key, (), max(1, total - bound), min(bound, total - 1) + 1)
        return jnp.stack([one, total - one])
    lengths = jnp.asarray(profile(amount, total, bound, lean), jnp.int32)
    twos = (amount - 1) // 2
    donor, receiver = lengths[1:1 + 2 * twos:2], lengths[2:2 + 2 * twos:2]
    room = jnp.minimum(donor - 1, bound - receiver)
    moved = jax.random.randint(jax.random.fold_in(own_key, 1), (twos,), 0, 1 << 20) % (room + 1)
    lengths = lengths.at[1:1 + 2 * twos:2].set(donor - moved).at[2:2 + 2 * twos:2].set(receiver + moved)
    return lengths[jax.random.permutation(jax.random.fold_in(own_key, 2), amount)]


def shared_out(rng, own, number, rows, count, top, most, slope):
    order = jax.random.permutation(rng, count)
    crowded, usual = load_shares(count, rows * top, most, slope, True), load_shares(count, rows * top, most, slope, False)
    places = jnp.arange(count)

    def named(sizes, offset_by):
        used = int((sizes > 0).sum())
        fixed = max(1, used // 4)
        shifted = fixed + (places - fixed + offset_by * (used - fixed)) % max(1, count - fixed)
        return jnp.zeros((count,), jnp.int32).at[order[jnp.where(places < fixed, places, shifted)]].set(jnp.asarray(sizes, jnp.int32))

    sizes = jnp.where(number % 4 == 0, named(crowded, number // 4), named(usual, number - number // 4 - 1))
    mixed = jax.random.permutation(jax.random.fold_in(own, 3), count)
    source_of, taker = mixed[0:count // 2 * 2:2], mixed[1:count // 2 * 2:2]
    margin = jnp.minimum(sizes[source_of] - 1, most - sizes[taker]) // 2
    margin = jnp.where((source_of == order[0]) | (taker == order[0]) | (sizes[taker] == 0), 0, jnp.maximum(margin, 0))
    shifted = jax.random.randint(jax.random.fold_in(own, 4), (count // 2,), 0, 1 << 20) % (margin + 1)
    sizes = sizes.at[source_of].add(-shifted).at[taker].add(shifted)
    members = jnp.searchsorted(jnp.cumsum(sizes), jnp.arange(rows * top), side="right").astype(jnp.int32)
    table = members.reshape(top, rows).T
    table = table[jax.random.permutation(jax.random.fold_in(own, 1), rows)]
    offset_by = jax.random.randint(jax.random.fold_in(own, 2), (rows, 1), 0, top)
    return jnp.take_along_axis(table, (jnp.arange(top)[None, :] + offset_by) % top, axis=1)


def load_shares(count, total, reach, slope, full):
    portions = [(1 << 20) // math.isqrt(rank ** slope) + 1 for rank in range(1, count + 1)]
    largest = reach if full else min(reach, max(-(-total // count), total * portions[0] // sum(portions)))
    least = 1 if total - largest >= count - 1 else 0
    holding, spare = [largest] + [least] * (count - 1), total - largest - least * (count - 1)
    while spare > 0:
        candidates = [i for i in range(1, count) if holding[i] < largest] or [i for i in range(1, count) if holding[i] < reach]
        mass, remaining = sum([portions[i] for i in candidates]), spare
        for i in candidates:
            addition = min(reach - holding[i], max(1, remaining * portions[i] // mass), spare)
            holding[i] = holding[i] + addition
            spare = spare - addition
    return np.array(holding)


def noise(own_key, shape, scale, reach, pieces=(), kind=jnp.bfloat16):
    array = jax.random.normal(own_key, shape, jnp.float32) * scale
    if len(pieces) > 0:
        array = block_scale(own_key, shape, pieces, -0.22, 0.18) * array
    return jnp.clip(array, min=-reach, max=reach).astype(kind)


def setup_inputs(seed: int = 0) -> dict:
    arg_keys = jax.random.split(jax.random.key(seed), 13)
    queries = draw_queries(jax.random.fold_in(arg_keys[12], 71), 0)
    enc_keys = draw_enc_keys(jax.random.fold_in(arg_keys[12], 71), 0)
    enc_values = noise(arg_keys[2], (SEQS, SRC_LEN, D), 8.0, 48.0, ((0, 32), (2, 16)))
    source_lengths = uneven(arg_keys[3], SEQS, SEQS * SRC_LEN // 2, SRC_LEN, 2).astype(jnp.int32)
    out_proj = noise(arg_keys[4], (D, D), D ** -0.5, 0.125, ((0, 16),))
    dec_state = draw_dec_state(jax.random.fold_in(arg_keys[12], 71), 0)
    norm_gain = jnp.clip(1.0 + 0.15 * jax.random.normal(arg_keys[6], (D,), jnp.float32), 0.25, 1.75)
    norm_bias = noise(arg_keys[7], (D,), 0.5, 3.0, ((0, 16),), jnp.float32)
    head_weight = draw_head_weight(jax.random.fold_in(arg_keys[12], 71), 0)
    shortlist_keys = jax.random.split(jax.random.fold_in(arg_keys[9], 1), TGT_ROWS // ROWS_DEV)
    shortlist_turns = jax.random.permutation(jax.random.fold_in(arg_keys[9], 3), TGT_ROWS // ROWS_DEV)
    shortlist = jax.vmap(lambda own, number: shared_out(jax.random.fold_in(arg_keys[9], 2), own, number, ROWS_DEV, VOCAB_BLOCKS, K_LIST, MOST, 2))(shortlist_keys, shortlist_turns).reshape((TGT_ROWS, K_LIST))
    target_slot = with_ends(jax.random.randint(arg_keys[10], (TGT_ROWS,), 0, K_LIST), jax.random.fold_in(arg_keys[10], 1), 0, K_LIST - 1).astype(jnp.int32)
    target_offset = with_ends(jax.random.randint(arg_keys[11], (TGT_ROWS,), 0, BLK), jax.random.fold_in(arg_keys[11], 1), 0, BLK - 1).astype(jnp.int32)
    return {"queries": queries, "enc_keys": enc_keys, "enc_values": enc_values, "source_lengths": source_lengths, "out_proj": out_proj, "dec_state": dec_state, "norm_gain": norm_gain, "norm_bias": norm_bias, "head_weight": head_weight, "shortlist": shortlist, "target_slot": target_slot, "target_offset": target_offset}


MASKED = -1e+30
EPSILON = 1e-05

def attend_sequence(inputs):
    query_rows, key_rows, value_rows, length = inputs
    scaling = 1.0 / math.sqrt(HD)
    queries_f = query_rows.reshape(ROWS_DEV, H, HD).astype(jnp.float32)
    keys_f = key_rows.reshape(SRC_LEN, H, HD).astype(jnp.float32)
    values_f = value_rows.reshape(SRC_LEN, H, HD).astype(jnp.float32)
    scores = jnp.einsum('rhe,phe->hrp', queries_f, keys_f) * scaling
    usable = (jnp.arange(SRC_LEN, dtype=jnp.int32) < length)[None, None, :]
    scores = jnp.where(usable, scores, MASKED)
    row_top = lax.optimization_barrier(jnp.max(scores, axis=-1, keepdims=True))
    raw_weights = jnp.where(usable, jnp.exp(scores - row_top), 0.0)
    totals = lax.optimization_barrier(jnp.sum(raw_weights, axis=-1))
    rounded = lax.optimization_barrier(raw_weights.astype(jnp.bfloat16)).astype(jnp.float32)
    mixture = jnp.einsum('hrp,phe->rhe', rounded, values_f)
    return (mixture / totals.T[:, :, None]).astype(jnp.bfloat16).reshape(ROWS_DEV, D)

def reference(queries, enc_keys, enc_values, source_lengths, out_proj, dec_state, norm_gain, norm_bias, head_weight, shortlist, target_slot, target_offset):
    attended = lax.map(attend_sequence, (queries.reshape(SEQS, ROWS_DEV, D), enc_keys, enc_values, source_lengths))
    attended = attended.reshape(TGT_ROWS, D)
    residual = dec_state.astype(jnp.float32) + jnp.dot(attended, out_proj, preferred_element_type=jnp.float32)
    row_mean = lax.optimization_barrier(jnp.mean(residual, axis=1, keepdims=True))
    variance = lax.optimization_barrier(jnp.mean((residual - row_mean) ** 2, axis=1, keepdims=True))
    inv_std = lax.rsqrt(variance + EPSILON)
    centered = (residual - row_mean) * inv_std
    normed = lax.optimization_barrier((centered * norm_gain + norm_bias).astype(jnp.bfloat16))
    columns = head_weight.reshape(D, VOCAB_BLOCKS, BLK)

    def score_rows(inputs):
        normed_rows, listed, slot_rows, offset_rows = inputs
        picked_cols = jnp.take(columns, listed, axis=1).astype(jnp.float32)
        logits = jnp.einsum('rd,drkt->rkt', normed_rows.astype(jnp.float32), picked_cols)
        row_best = lax.optimization_barrier(jnp.max(logits, axis=(1, 2)))
        log_total = row_best + jnp.log(lax.optimization_barrier(jnp.sum(jnp.exp(logits - row_best[:, None, None]), axis=(1, 2))))
        list_hit = jnp.arange(K_LIST, dtype=jnp.int32)[None, :, None] == slot_rows[:, None, None]
        place_hit = jnp.arange(BLK, dtype=jnp.int32)[None, None, :] == offset_rows[:, None, None]
        target_hit = jnp.logical_and(list_hit, place_hit)
        chosen = lax.optimization_barrier(jnp.sum(jnp.where(target_hit, logits, 0.0), axis=(1, 2)))
        deltas = jnp.exp(logits - log_total[:, None, None]) - target_hit.astype(jnp.float32)
        deltas = lax.optimization_barrier(deltas.astype(jnp.bfloat16)).astype(jnp.float32)
        grads = jnp.einsum('rkt,drkt->rd', deltas, picked_cols)
        return (log_total - chosen, grads)
    group_count = TGT_ROWS // 8
    losses, grad_normed = lax.map(score_rows, (normed.reshape(group_count, 8, D), shortlist.reshape(group_count, 8, K_LIST), target_slot.reshape(group_count, 8), target_offset.reshape(group_count, 8)))
    row_loss = losses.reshape(TGT_ROWS)
    grad_normed = grad_normed.reshape(TGT_ROWS, D)
    gained = grad_normed * norm_gain
    mean_g = lax.optimization_barrier(jnp.mean(gained, axis=1, keepdims=True))
    mean_gx = lax.optimization_barrier(jnp.mean(gained * centered, axis=1, keepdims=True))
    grad_state = inv_std * (gained - mean_g - centered * mean_gx)
    return (row_loss, grad_state)
```

```python
import math

import jax
import jax.numpy as jnp
from jax import lax
from jax.experimental import pallas as pl
from jax.experimental.pallas import tpu as pltpu
from jax.sharding import PartitionSpec as P

HD = 128
BLK = 128
MOST = 2
EPSILON = 1e-05
MASKED = -1e30
F32 = jnp.float32
BF16 = jnp.bfloat16
I32 = jnp.int32

VM = pl.BlockSpec(memory_space=pltpu.VMEM)
SM = pl.BlockSpec(memory_space=pltpu.SMEM)


def call(body, outs, specs, scratch=(), name=None):
    return pl.pallas_call(
        body,
        out_shape=tuple(jax.ShapeDtypeStruct(s, d) for s, d in outs),
        in_specs=specs,
        out_specs=tuple(VM for _ in outs),
        scratch_shapes=list(scratch),
        name=name,
    )


def dot(a, b, ca, cb):
    return lax.dot_general(a, b, (((ca,), (cb,)), ((), ())), preferred_element_type=F32)


def thirds(x):
    hi = x.astype(BF16)
    rest = x - hi.astype(F32)
    mid = rest.astype(BF16)
    low = (rest - mid.astype(F32)).astype(BF16)
    return hi, mid, low


def pack_kernel(head_ref, wsend_ref):
    groups, width, tokens = wsend_ref.shape
    last = head_ref.shape[1] - (groups - 1) * tokens
    for u in range(groups - 1):
        wsend_ref[u] = head_ref[:, u * tokens : (u + 1) * tokens]
    wsend_ref[groups - 1, :, :last] = head_ref[:, (groups - 1) * tokens :]
    if last < tokens:
        wsend_ref[groups - 1, :, last:] = jnp.zeros((width, tokens - last), BF16)


def slots_kernel(where_ref, list_ref, tslot_ref, toff_ref, m_ref, mj_ref, code_ref, *, blocks, group, most):
    pieces = group * most
    slots, rows = m_ref.shape
    vocs = code_ref.shape[0] // pieces
    listed = list_ref[...]
    picks = listed.shape[0]
    r0 = lax.broadcasted_iota(I32, (rows, rows), 0)
    r1 = lax.broadcasted_iota(I32, (rows, rows), 1)
    earlier = (r0 < r1).astype(F32).astype(BF16)
    tslot = tslot_ref[...]
    target_block = jnp.zeros((1, rows), I32)
    for k in range(picks):
        target_block = jnp.where(tslot == k, listed[k : k + 1, :], target_block)

    def mask_of(u, v, j):
        local = u * group + lax.rem(j, group)
        block = jnp.where(local < blocks, v * blocks + local, -1)
        named = block == listed[0:1, :]
        for k in range(1, picks):
            named = jnp.logical_or(named, block == listed[k : k + 1, :])
        named = named.astype(F32)
        rank = dot(named.astype(BF16), earlier, 1, 0)
        want = lax.div(j, group).astype(F32)
        return jnp.where(rank == want, named, 0.0), block

    step = 512
    span = vocs * pieces
    sub = lax.broadcasted_iota(I32, (step, 1), 0)

    def travel(t, carry):
        i = t * step + sub
        u = lax.div(i, span)
        v = lax.div(lax.rem(i, span), pieces)
        j = lax.rem(i, pieces)
        m, _ = mask_of(u, v, j)
        m_ref[pl.ds(pl.multiple_of(t * step, step), step), :] = m.astype(BF16)
        return carry

    lax.fori_loop(0, slots // step, travel, 0)
    pairs = slots // pieces

    def major(t, carry):
        w = lax.broadcasted_iota(I32, (pairs, 1), 0)
        m, _ = mask_of(lax.div(w, vocs), lax.rem(w, vocs), jnp.full((pairs, 1), t, I32))
        mj_ref[t] = m.astype(BF16)
        return carry

    lax.fori_loop(0, pieces, major, 0)

    i = lax.broadcasted_iota(I32, (span, 1), 0)
    m, block = mask_of(jnp.full((span, 1), where_ref[0], I32), lax.div(i, pieces), lax.rem(i, pieces))
    hit = jnp.where(block == target_block, toff_ref[...].astype(F32) + 1.0, 0.0)
    code = jnp.sum(m * (hit + 1.0), axis=1, keepdims=True) - 2.0
    code_ref[...] = jnp.broadcast_to(code, code_ref.shape)


EXTRA = 16


def attend_kernel(len_ref, q_ref, k_ref, v_ref, proj_ref, dec_ref, gain_ref, bias_ref, out_ref):
    groups, _, width = out_ref.shape
    rows = q_ref.shape[0]
    scores = dot(q_ref[...], k_ref[0], 1, 1) * (1.0 / math.sqrt(HD))
    usable = lax.broadcasted_iota(I32, scores.shape, 1) < len_ref[0]
    scores = jnp.where(usable, scores, MASKED)
    top = jnp.max(scores, axis=1, keepdims=True)
    raw = jnp.where(usable, jnp.exp(scores - top), 0.0)
    totals = jnp.sum(raw, axis=1, keepdims=True)
    mixed = dot(raw.astype(BF16), v_ref[0], 1, 0)
    att = (mixed / totals).astype(BF16)
    proj_sums = jnp.zeros((8, width), F32)
    ones = jnp.ones((8, width), BF16)
    for u in range(groups):
        piece = proj_ref[:, u * width : (u + 1) * width]
        out_ref[u, :rows, :] = dot(att, piece, 1, 0).astype(BF16)
        proj_sums = proj_sums + dot(ones, piece, 1, 1)
    part = dot(ones, dec_ref[...], 1, 1)
    for third in thirds(proj_sums):
        part = part + dot(third, att, 1, 1)
    sub = lax.broadcasted_iota(I32, (EXTRA, width), 0)
    extra = jnp.zeros((EXTRA, width), F32)
    lines = []
    for third in thirds(part[0:1, :]):
        lines += [third[:, c * 128 : (c + 1) * 128] for c in range(rows // 128)]
    lines += list(thirds(gain_ref[...])) + list(thirds(bias_ref[...]))
    for n, line in enumerate(lines):
        extra = jnp.where(sub == n, line.astype(F32), extra)
    extra = extra.astype(BF16)
    for u in range(groups):
        out_ref[u, rows:, :] = extra


def residual_kernel(part_ref, dec_ref, gain_ref, m_ref, c_ref, extra_ref, out_ref):
    groups, _, width = part_ref.shape
    rows = dec_ref.shape[0]
    acc = dec_ref[...].astype(F32)
    lines = jnp.zeros((EXTRA, width), F32)
    for u in range(groups):
        acc = acc + part_ref[u, :rows, :].astype(F32)
        lines = lines + part_ref[u, rows:, :].astype(F32)
        extra_ref[u] = part_ref[u, rows:, :]
    n = rows // 128
    halves = []
    for c in range(n):
        line = lines[c : c + 1] + lines[n + c : n + c + 1] + lines[2 * n + c : 2 * n + c + 1]
        halves.append(jnp.transpose(jnp.broadcast_to(line, (8, 128)))[:, 0:1])
    mean = jnp.concatenate(halves, axis=0) / (groups * width)
    c = acc - mean
    c_ref[...] = c
    x = (c * gain_ref[...]).astype(BF16)
    out_ref[...] = dot(m_ref[...], x, 1, 0).astype(BF16)


def spread_lanes(cols, shape):
    lane = lax.broadcasted_iota(I32, shape, 1)
    out = jnp.zeros(shape, F32)
    for n, col in enumerate(cols):
        out = jnp.where(lane == n, col, out)
    return out


STATS = 8


def score_kernel(x_ref, w_ref, extra_ref, code_ref, l_ref, row_ref, stat_ref, *, group, lines):
    groups, slots, width = x_ref.shape
    pieces = 2 * group
    tokens = group * BLK
    acc = jnp.zeros((slots, tokens), F32)
    sums = jnp.zeros((EXTRA, tokens), F32)
    squares = jnp.zeros((slots, width), F32)
    for u in range(groups):
        x = x_ref[u]
        w = w_ref[u]
        acc = acc + dot(x, w, 1, 0)
        small = extra_ref[u]
        gain = small.astype(F32)
        gain = gain[lines : lines + 1] + gain[lines + 1 : lines + 2] + gain[lines + 2 : lines + 3]
        plain = x.astype(F32) / gain
        squares = squares + plain * plain
        sums = sums + dot(small, w, 1, 0)
    wg = sums[lines : lines + 1] + sums[lines + 1 : lines + 2] + sums[lines + 2 : lines + 3]
    wb = sums[lines + 3 : lines + 4] + sums[lines + 4 : lines + 5] + sums[lines + 5 : lines + 6]
    inv = lax.rsqrt(jnp.sum(squares, axis=1, keepdims=True) / (groups * width) + EPSILON)
    place = lax.rem(lax.broadcasted_iota(I32, (slots, 1), 0), group)
    dots = acc[:, 0:BLK]
    gains = jnp.broadcast_to(wg[:, 0:BLK], dots.shape)
    biases = jnp.broadcast_to(wb[:, 0:BLK], dots.shape)
    for b in range(1, group):
        here = place == b
        cut = slice(b * BLK, (b + 1) * BLK)
        dots = jnp.where(here, acc[:, cut], dots)
        gains = jnp.where(here, wg[:, cut], gains)
        biases = jnp.where(here, wb[:, cut], biases)
    bare = inv * dots
    logits = bare + biases
    l_ref[...] = logits
    top = jnp.max(logits, axis=1, keepdims=True)
    shifted = jnp.exp(logits - top)
    spread = jnp.sum(shifted, axis=1, keepdims=True)
    lse = top + jnp.log(spread)
    soft = shifted / spread
    lane = lax.broadcasted_iota(I32, logits.shape, 1).astype(F32)
    hit = lane == code_ref[...]

    def row_sum(v):
        return jnp.sum(v, axis=1, keepdims=True)

    stat_ref[...] = spread_lanes(
        [
            lse,
            row_sum(jnp.where(hit, logits, 0.0)),
            inv,
            row_sum(soft * gains),
            row_sum(soft * bare),
            row_sum(jnp.where(hit, gains, 0.0)),
            row_sum(jnp.where(hit, bare, 0.0)),
        ],
        logits.shape,
    )
    sents = slots // pieces
    lane_s = lax.broadcasted_iota(I32, (sents, 128), 1)
    packed = jnp.zeros((sents, 128), F32)
    for j in range(pieces):
        z = stat_ref[pl.ds(j, sents, stride=pieces), :]
        if j:
            z = pltpu.roll(z, j * STATS, 1)
        packed = jnp.where(lane_s // STATS == j, z, packed)
    for u in range(groups):
        row_ref[u * sents : (u + 1) * sents, :] = packed


def total_kernel(where_ref, e_ref, mj_ref, m_ref, tot_ref, loss_ref, back_ref):
    pieces, pairs, rows = mj_ref.shape
    low = jnp.full((1, rows), MASKED, F32)
    for j in range(pieces):
        lse = e_ref[:, j * STATS : j * STATS + 1]
        low = jnp.maximum(low, jnp.max(jnp.where(mj_ref[j].astype(F32) > 0.0, lse, MASKED), axis=0, keepdims=True))
    total = jnp.zeros((1, rows), F32)
    picked = jnp.zeros((1, rows), F32)
    for j in range(pieces):
        there = mj_ref[j].astype(F32) > 0.0
        lse = e_ref[:, j * STATS : j * STATS + 1]
        pick = e_ref[:, j * STATS + 1 : j * STATS + 2]
        total = total + jnp.sum(jnp.where(there, jnp.exp(lse - low), 0.0), axis=0, keepdims=True)
        picked = picked + jnp.sum(jnp.where(there, pick, 0.0), axis=0, keepdims=True)
    log_total = low + jnp.log(total)
    tot_ref[...] = jnp.broadcast_to(log_total, tot_ref.shape)
    loss_ref[...] = log_total - picked
    slots = back_ref.shape[0]
    own = m_ref[pl.ds(pl.multiple_of(where_ref[0] * slots, slots), slots), :].astype(F32)
    back_ref[...] = jnp.broadcast_to(jnp.sum(own * log_total, axis=1, keepdims=True), back_ref.shape)


def delta_kernel(l_ref, code_ref, back_ref, w_ref, out_ref, *, group):
    groups, width, tokens = w_ref.shape
    logits = l_ref[...]
    code = code_ref[...]
    lane = lax.broadcasted_iota(I32, logits.shape, 1).astype(F32)
    deltas = jnp.exp(logits - back_ref[...]) - jnp.where(lane == code, 1.0, 0.0)
    deltas = jnp.where(code > -1.5, deltas, 0.0)
    place = lax.rem(lax.broadcasted_iota(I32, logits.shape, 0), group)
    wide = jnp.concatenate([jnp.where(place == b, deltas, 0.0) for b in range(group)], axis=1).astype(BF16)
    for u in range(groups):
        out_ref[u] = dot(wide, w_ref[u], 1, 1).astype(BF16)


def sums_kernel(e_ref, mj_ref, tot_ref, out_ref):
    pieces, pairs, rows = mj_ref.shape
    log_total = tot_ref[0:1, :]
    sum_g = jnp.zeros((1, rows), F32)
    sum_gx = jnp.zeros((1, rows), F32)
    inv = jnp.zeros((1, rows), F32)
    for j in range(pieces):
        there = mj_ref[j].astype(F32) > 0.0

        def col(n):
            return e_ref[:, j * STATS + n : j * STATS + n + 1]

        share = jnp.where(there, jnp.exp(col(0) - log_total), 0.0)
        sum_g = sum_g + jnp.sum(jnp.where(there, share * col(3) - col(5), 0.0), axis=0, keepdims=True)
        sum_gx = sum_gx + jnp.sum(jnp.where(there, share * col(4) - col(6), 0.0), axis=0, keepdims=True)
        inv = jnp.maximum(inv, jnp.max(jnp.where(there, col(2), 0.0), axis=0, keepdims=True))
    sub = lax.broadcasted_iota(I32, (8, rows), 0)
    out = jnp.where(sub == 0, sum_g, jnp.where(sub == 1, sum_gx, inv))
    out_ref[...] = out


def final_kernel(r_ref, m_ref, c_ref, gain_ref, sums_ref, out_ref, *, total):
    grad = dot(m_ref[...], r_ref[...], 0, 0)
    rows = grad.shape[0]
    cols = jnp.concatenate(
        [jnp.transpose(sums_ref[:, c * 128 : (c + 1) * 128])[:, 0:3] for c in range(rows // 128)], axis=0
    )
    inv = cols[:, 2:3]
    g = grad * gain_ref[...]
    centered = c_ref[...] * inv
    out_ref[...] = inv * (g - cols[:, 0:1] / total - centered * (cols[:, 1:2] / total))


def shards(
    queries,
    enc_keys,
    enc_values,
    source_lengths,
    out_proj,
    dec_state,
    norm_gain,
    norm_bias,
    head_weight,
    shortlist,
    target_slot,
    target_offset,
):
    vocs = lax.axis_size("vocab")
    groups = lax.axis_size("src")
    both = ("src", "vocab")
    rows, width = dec_state.shape
    total = out_proj.shape[1]
    blocks = head_weight.shape[1] // BLK
    group = -(-blocks // groups)
    tokens = group * BLK
    pieces = group * MOST
    pairs = groups * vocs
    slots = pairs * pieces
    here = lax.axis_index("src").reshape(1).astype(I32)
    gain = norm_gain.reshape(1, width)
    bias = norm_bias.reshape(1, width)

    def exchange(x, axis):
        return lax.all_to_all(x, axis, split_axis=0, concat_axis=0, tiled=True)

    (parts,) = call(attend_kernel, [((groups, rows + EXTRA, width), BF16)], [SM] + [VM] * 7, name="attend")(
        source_lengths, queries, enc_keys, enc_values, out_proj, dec_state, gain, bias
    )
    parts = exchange(parts, "src")
    (wsend,) = call(pack_kernel, [((groups, width, tokens), BF16)], [VM], name="pack")(head_weight)
    win = exchange(wsend, "src")
    m, mj, code = call(
        lambda *refs: slots_kernel(*refs, blocks=blocks, group=group, most=MOST),
        [((slots, rows), BF16), ((pieces, pairs, rows), BF16), ((vocs * pieces, 128), F32)],
        [SM, VM, VM, VM],
        name="slots",
    )(here, shortlist.T, target_slot.reshape(1, rows), target_offset.reshape(1, rows))
    codes = exchange(code.reshape(vocs, pieces, 128), "vocab").reshape(vocs * pieces, 128)
    c, extras, outgoing = call(
        residual_kernel,
        [((rows, width), F32), ((groups, EXTRA, width), BF16), ((slots, width), BF16)],
        [VM] * 4,
        name="residual",
    )(parts, dec_state, gain, m)
    incoming = exchange(outgoing.reshape(pairs, pieces, width), both)
    logits, stats = call(
        lambda *refs: score_kernel(*refs, group=group, lines=3 * (rows // 128)),
        [((vocs * pieces, BLK), F32), ((pairs, 128), F32)],
        [VM] * 4,
        scratch=[pltpu.VMEM((vocs * pieces, BLK), F32)],
        name="score",
    )(incoming.reshape(groups, vocs * pieces, width), win, extras, codes)
    back_stats = exchange(stats.reshape(pairs, 1, 128), both).reshape(pairs, 128)
    totals, loss, back = call(
        total_kernel,
        [((8, rows), F32), ((1, rows), F32), ((vocs * pieces, 128), F32)],
        [SM, VM, VM, VM],
        name="total",
    )(here, back_stats, mj, m)
    back_in = exchange(back.reshape(vocs, pieces, 128), "vocab").reshape(vocs * pieces, 128)
    (grads,) = call(
        lambda *refs: delta_kernel(*refs, group=group),
        [((groups, vocs * pieces, width), BF16)],
        [VM] * 4,
        name="delta",
    )(logits, codes, back_in, win)
    returned = exchange(grads.reshape(pairs, pieces, width), both).reshape(slots, width)
    (sums,) = call(sums_kernel, [((8, rows), F32)], [VM] * 3, name="sums")(back_stats, mj, totals)
    (grad_state,) = call(
        lambda *refs: final_kernel(*refs, total=total), [((rows, width), F32)], [VM] * 5, name="final"
    )(returned, m, c, gain, sums)
    return (loss.reshape(rows), grad_state)


def solution(mesh):
    placed = (
        P("vocab", "src"),
        P("vocab", None, "src"),
        P("vocab", None, "src"),
        P("vocab"),
        P("src", None),
        P("vocab", "src"),
        P("src"),
        P("src"),
        P("src", "vocab"),
        P("vocab", None),
        P("vocab"),
        P("vocab"),
    )
    return jax.shard_map(
        shards,
        mesh=mesh,
        in_specs=placed,
        out_specs=(P("vocab"), P("vocab", "src")),
        check_vma=False,
    )
```

```python
import math

import jax
import jax.numpy as jnp
from jax import lax
from jax.experimental import pallas as pl
from jax.experimental.pallas import tpu as pltpu
from jax.sharding import Mesh
from jax.sharding import PartitionSpec as P


HD = 128
BLK = 128
MOST = 2
EPSILON = 1e-05
MASKED = -1e30
F32 = jnp.float32
BF16 = jnp.bfloat16
I32 = jnp.int32

VM = pl.BlockSpec(memory_space=pltpu.VMEM)
SM = pl.BlockSpec(memory_space=pltpu.SMEM)
CORES = 2
STATS = 8
EXTRA = 16


def call(body, outs, specs, scratch=()):
    return pl.pallas_call(
        body,
        out_shape=tuple(jax.ShapeDtypeStruct(s, d) for s, d in outs),
        in_specs=specs,
        out_specs=tuple(VM for _ in outs),
        scratch_shapes=list(scratch),
    )


def dot(a, b, ca, cb):
    return lax.dot_general(a, b, (((ca,), (cb,)), ((), ())), preferred_element_type=F32)


def thirds(x):
    hi = x.astype(BF16)
    rest = x - hi.astype(F32)
    mid = rest.astype(BF16)
    low = (rest - mid.astype(F32)).astype(BF16)
    return hi, mid, low


def stack_rows(lines, count, width):
    sub = lax.broadcasted_iota(I32, (count, width), 0)
    out = jnp.zeros((count, width), F32)
    for n, line in enumerate(lines):
        out = jnp.where(sub == n, line.astype(F32), out)
    return out


def pack_kernel(where_ref, head_ref, *out_refs):
    chips = len(out_refs)
    _, tokens = out_refs[0].shape
    cols = head_ref.shape[1]
    for o in range(chips):
        to = lax.rem(where_ref[0] + o, chips)
        start = pl.multiple_of(to * tokens, BLK)
        for t in range(tokens // BLK):
            first = start + t * BLK
            there = first < cols
            safe = pl.multiple_of(jnp.minimum(first, cols - BLK), BLK)
            piece = head_ref[:, pl.ds(safe, BLK)]
            out_refs[o][:, t * BLK : (t + 1) * BLK] = jnp.where(there, piece, jnp.zeros_like(piece))


def share_kernel(where_ref, q_ref, k_ref, v_ref, proj_ref, dec_ref, out_ref):
    rows, width = q_ref.shape
    mem = k_ref.shape[1]
    chips = proj_ref.shape[1] // (CORES * width)
    other = 1 - where_ref[1]
    out_ref[0:rows, :] = q_ref[...]
    out_ref[rows : rows + mem, :] = k_ref[0]
    out_ref[rows + mem : rows + 2 * mem, :] = v_ref[0]
    base = rows + 2 * mem
    for y in range(chips):
        cols = pl.ds(pl.multiple_of((y * CORES + other) * width, width), width)
        out_ref[base + y * width : base + (y + 1) * width, :] = proj_ref[:, cols]
    base = base + chips * width
    sums = dot(jnp.ones((8, proj_ref.shape[1]), BF16), proj_ref[...], 1, 1)
    dec_sums = dot(jnp.ones((8, width), BF16), dec_ref[...], 1, 1)
    lines = list(thirds(sums[0:1, :]))
    for third in thirds(dec_sums[0:1, :]):
        lines += [third[:, c * 128 : (c + 1) * 128] for c in range(rows // 128)]
    out_ref[base:, :] = stack_rows(lines, EXTRA, width).astype(BF16)


def mask_of(listed, earlier, u, v, j, blocks, group):
    local = u * group + lax.rem(j, group)
    block = jnp.where(local < blocks, v * blocks + local, -1)
    named = block == listed[0:1, :]
    for k in range(1, listed.shape[0]):
        named = jnp.logical_or(named, block == listed[k : k + 1, :])
    named = named.astype(F32)
    rank = dot(named.astype(BF16), earlier, 1, 0)
    return jnp.where(rank == lax.div(j, group).astype(F32), named, 0.0), block


def earlier_of(rows):
    r0 = lax.broadcasted_iota(I32, (rows, rows), 0)
    r1 = lax.broadcasted_iota(I32, (rows, rows), 1)
    return (r0 < r1).astype(F32).astype(BF16)


def code_kernel(where_ref, list_ref, tslot_ref, toff_ref, code_ref, *, blocks, group):
    pieces = group * MOST
    span = code_ref.shape[0]
    listed = list_ref[...]
    tslot = tslot_ref[...]
    rows = listed.shape[1]
    target_block = jnp.zeros((1, rows), I32)
    for k in range(listed.shape[0]):
        target_block = jnp.where(tslot == k, listed[k : k + 1, :], target_block)
    i = lax.broadcasted_iota(I32, (span, 1), 0)
    u = jnp.full((span, 1), where_ref[0], I32)
    m, block = mask_of(listed, earlier_of(rows), u, lax.div(i, pieces), lax.rem(i, pieces), blocks, group)
    hit = jnp.where(block == target_block, toff_ref[...].astype(F32) + 1.0, 0.0)
    code = jnp.sum(m * (hit + 1.0), axis=1, keepdims=True) - 2.0
    code_ref[...] = jnp.broadcast_to(code, code_ref.shape).astype(BF16)


def slots_kernel(list_ref, m_ref, mj_ref, *, blocks, group, vocs):
    pieces = group * MOST
    slots, rows = m_ref.shape
    pairs = slots // pieces
    listed = list_ref[...]
    earlier = earlier_of(rows)
    step = 256
    span = vocs * pieces
    sub = lax.broadcasted_iota(I32, (step, 1), 0)

    def travel(t, carry):
        i = t * step + sub
        u = lax.div(i, span)
        v = lax.div(lax.rem(i, span), pieces)
        m, _ = mask_of(listed, earlier, u, v, lax.rem(i, pieces), blocks, group)
        m_ref[pl.ds(pl.multiple_of(t * step, step), step), :] = m.astype(BF16)
        return carry

    lax.fori_loop(0, slots // step, travel, 0)
    w = lax.broadcasted_iota(I32, (pairs, 1), 0)

    def major(t, carry):
        j = jnp.full((pairs, 1), t, I32)
        m, _ = mask_of(listed, earlier, lax.div(w, vocs), lax.rem(w, vocs), j, blocks, group)
        mj_ref[t] = m.astype(BF16)
        return carry

    lax.fori_loop(0, pieces, major, 0)


def whole_line(lines, first, n):
    cut = [lines[first + i : first + i + 1] for i in range(3 * n)]
    return jnp.concatenate([cut[c] + cut[n + c] + cut[2 * n + c] for c in range(n)], axis=1)


def attend(q, k, v, length):
    scores = dot(q, k, 1, 1) * (1.0 / math.sqrt(HD))
    usable = lax.broadcasted_iota(I32, scores.shape, 1) < length
    scores = jnp.where(usable, scores, MASKED)
    top = jnp.max(scores, axis=1, keepdims=True)
    raw = jnp.where(usable, jnp.exp(scores - top), 0.0)
    totals = jnp.sum(raw, axis=1, keepdims=True)
    return (dot(raw.astype(BF16), v, 1, 0) / totals).astype(BF16)


def attend_kernel(
    where_ref, len_ref, q_ref, k_ref, v_ref, proj_ref, dec_ref, gain_ref, bias_ref, other_ref, out_ref
):
    chips, _, width = out_ref.shape
    rows = q_ref.shape[0]
    mem = k_ref.shape[1]
    core = where_ref[1]
    length = len_ref[0]
    att = attend(q_ref[...], k_ref[0], v_ref[0], length)
    q2, k2, v2 = other_ref[0:rows, :], other_ref[rows : rows + mem, :], other_ref[rows + mem : rows + 2 * mem, :]
    att2 = attend(q2, k2, v2, length)
    base = rows + 2 * mem
    for y in range(chips):
        own = proj_ref[:, pl.ds(pl.multiple_of((y * CORES + core) * width, width), width)]
        out_ref[y, :rows, :] = (
            dot(att, own, 1, 0) + dot(att2, other_ref[base + y * width : base + (y + 1) * width, :], 1, 0)
        ).astype(BF16)
    base = base + chips * width
    sums = dot(jnp.ones((8, proj_ref.shape[1]), BF16), proj_ref[...], 1, 1)
    part = dot(jnp.ones((8, width), BF16), dec_ref[...], 1, 1)
    for third in thirds(sums):
        part = part + dot(third, att, 1, 1)
    other_sums = dot(other_ref[base:, :], att2, 1, 1)
    line = part[0:1, :] + (other_sums[0:1, :] + other_sums[1:2, :] + other_sums[2:3, :])
    line = line + whole_line(other_ref[base:, :].astype(F32), 3, rows // 128)
    lines = []
    for third in thirds(line):
        lines += [third[:, c * 128 : (c + 1) * 128] for c in range(rows // 128)]
    lines += list(thirds(gain_ref[...])) + list(thirds(bias_ref[...]))
    extra = stack_rows(lines, EXTRA, width).astype(BF16)
    for y in range(chips):
        out_ref[y, rows:, :] = extra


def columns(line):
    n = line.shape[1] // 128
    parts = [jnp.transpose(jnp.broadcast_to(line[:, c * 128 : (c + 1) * 128], (8, 128)))[:, 0:1] for c in range(n)]
    return jnp.concatenate(parts, axis=0)


def residual_kernel(part_ref, dec_ref, gain_ref, m_ref, c_ref, extra_ref, out_ref, *, total):
    chips, _, width = part_ref.shape
    rows = dec_ref.shape[0]
    acc = dec_ref[...].astype(F32)
    lines = jnp.zeros((EXTRA, width), F32)
    for y in range(chips):
        acc = acc + part_ref[y, :rows, :].astype(F32)
        lines = lines + part_ref[y, rows:, :].astype(F32)
        extra_ref[y] = part_ref[y, rows:, :]
    line = whole_line(lines, 0, rows // 128)
    c = acc - columns(line) / total
    c_ref[...] = c
    x = (c * gain_ref[...]).astype(BF16)
    out_ref[...] = dot(m_ref[...], x, 1, 0).astype(BF16)


def third_sum(x, first):
    return x[first : first + 1] + x[first + 1 : first + 2] + x[first + 2 : first + 3]


def half_kernel(where_ref, x_ref, extra_ref, *refs, group, lines):
    w_refs, out_ref = refs[:-1], refs[-1]
    chips, slots, width = x_ref.shape
    tokens = group * BLK
    acc = jnp.zeros((slots, tokens), F32)
    sums = jnp.zeros((EXTRA, tokens), F32)
    squares = jnp.zeros((slots, width), F32)
    for o in range(chips):
        y = lax.rem(where_ref[0] + (chips - o), chips)
        x = x_ref[y]
        w = w_refs[o][...]
        acc = acc + dot(x, w, 1, 0)
        small = extra_ref[y]
        plain = x.astype(F32) / third_sum(small.astype(F32), lines)
        squares = squares + plain * plain
        sums = sums + dot(small, w, 1, 0)
    place = lax.rem(lax.broadcasted_iota(I32, (slots, 1), 0), group)
    dots = acc[:, 0:BLK]
    for b in range(1, group):
        dots = jnp.where(place == b, acc[:, b * BLK : (b + 1) * BLK], dots)
    out_ref[0:slots, :] = dots
    ones = jnp.ones((8, width), BF16)
    total = jnp.zeros((8, slots), F32)
    for third in thirds(squares):
        total = total + dot(ones, third, 1, 1)
    base = slots
    n = slots // 128
    for c in range(n):
        out_ref[base + c : base + c + 1, :] = total[0:1, c * 128 : (c + 1) * 128]
    base = base + n
    for first in (lines, lines + 3):
        line = third_sum(sums, first)
        for b in range(group):
            out_ref[base + b : base + b + 1, :] = line[:, b * BLK : (b + 1) * BLK]
        base = base + group
    if base < out_ref.shape[0]:
        out_ref[base:, :] = jnp.zeros((out_ref.shape[0] - base, BLK), F32)


def score_kernel(own_ref, other_ref, code_ref, l_ref, row_ref, stat_ref, *, group, total):
    slots = l_ref.shape[0]
    pieces = MOST * group
    both = own_ref[...] + other_ref[...]
    dots = both[0:slots]
    n = slots // 128
    squares = columns(jnp.concatenate([both[slots + c : slots + c + 1] for c in range(n)], axis=1))
    inv = lax.rsqrt(squares / total + EPSILON)
    place = lax.rem(lax.broadcasted_iota(I32, (slots, 1), 0), group)
    at = slots + n
    gains = jnp.broadcast_to(both[at : at + 1], dots.shape)
    biases = jnp.broadcast_to(both[at + group : at + group + 1], dots.shape)
    for b in range(1, group):
        gains = jnp.where(place == b, both[at + b : at + b + 1], gains)
        biases = jnp.where(place == b, both[at + group + b : at + group + b + 1], biases)
    bare = inv * dots
    logits = bare + biases
    l_ref[...] = logits
    top = jnp.max(logits, axis=1, keepdims=True)
    shifted = jnp.exp(logits - top)
    spread = jnp.sum(shifted, axis=1, keepdims=True)
    lse = top + jnp.log(spread)
    soft = shifted / spread
    lane = lax.broadcasted_iota(I32, logits.shape, 1)
    hit = lane.astype(F32) == code_ref[...].astype(F32)

    def row_sum(v):
        return jnp.sum(v, axis=1, keepdims=True)

    cols = [
        lse,
        row_sum(jnp.where(hit, logits, 0.0)),
        inv,
        row_sum(soft * gains),
        row_sum(soft * bare),
        row_sum(jnp.where(hit, gains, 0.0)),
        row_sum(jnp.where(hit, bare, 0.0)),
    ]
    out = jnp.zeros(logits.shape, F32)
    for n, col in enumerate(cols):
        out = jnp.where(lane == n, col, out)
    stat_ref[...] = out
    sents = slots // pieces
    lane_s = lax.div(lax.broadcasted_iota(I32, (sents, 128), 1), STATS)
    packed = jnp.zeros((sents, 128), F32)
    for j in range(pieces):
        z = stat_ref[pl.ds(j, sents, stride=pieces), :]
        if j:
            z = pltpu.roll(z, j * STATS, 1)
        packed = jnp.where(lane_s == j, z, packed)
    for u in range(row_ref.shape[0] // sents):
        row_ref[u * sents : (u + 1) * sents, :] = packed


def total_kernel(where_ref, e_ref, mj_ref, m_ref, tot_ref, loss_ref, back_ref):
    pieces, pairs, rows = mj_ref.shape
    low = jnp.full((8, rows), MASKED, F32)
    for j in range(pieces):
        lse = jnp.where(mj_ref[j].astype(F32) > 0.0, e_ref[:, j * STATS : j * STATS + 1], MASKED)
        low = jnp.maximum(low, jnp.max(lse.reshape(pairs // 8, 8, rows), axis=0))
    low = jnp.max(low, axis=0, keepdims=True)
    total = jnp.zeros((8, rows), F32)
    picked = jnp.zeros((8, rows), F32)
    for j in range(pieces):
        there = mj_ref[j].astype(F32) > 0.0
        lse = e_ref[:, j * STATS : j * STATS + 1]
        pick = e_ref[:, j * STATS + 1 : j * STATS + 2]
        total = total + jnp.sum(jnp.where(there, jnp.exp(lse - low), 0.0).reshape(pairs // 8, 8, rows), axis=0)
        picked = picked + jnp.sum(jnp.where(there, pick, 0.0).reshape(pairs // 8, 8, rows), axis=0)
    log_total = low + jnp.log(jnp.sum(total, axis=0, keepdims=True))
    tot_ref[...] = jnp.broadcast_to(log_total, tot_ref.shape)
    loss_ref[...] = log_total - jnp.sum(picked, axis=0, keepdims=True)
    slots = back_ref.shape[0]
    own = m_ref[pl.ds(pl.multiple_of(where_ref[0] * slots, slots), slots), :].astype(F32)
    back_ref[...] = jnp.broadcast_to(jnp.sum(own * log_total, axis=1, keepdims=True), back_ref.shape)


def delta_kernel(where_ref, l_ref, code_ref, back_ref, *refs, group):
    w_refs, out_ref = refs[:-1], refs[-1]
    chips = len(w_refs)
    logits = l_ref[...]
    code = code_ref[...].astype(F32)
    lane = lax.broadcasted_iota(I32, logits.shape, 1).astype(F32)
    deltas = jnp.exp(logits - back_ref[...]) - jnp.where(lane == code, 1.0, 0.0)
    deltas = jnp.where(code > -1.5, deltas, 0.0)
    place = lax.rem(lax.broadcasted_iota(I32, logits.shape, 0), group)
    wide = jnp.concatenate([jnp.where(place == b, deltas, 0.0).astype(BF16) for b in range(group)], axis=1)
    for o in range(chips):
        y = lax.rem(where_ref[0] + (chips - o), chips)
        out_ref[y] = dot(wide, w_refs[o][...], 1, 1).astype(BF16)


def sums_kernel(e_ref, mj_ref, tot_ref, out_ref):
    pieces, pairs, rows = mj_ref.shape
    log_total = tot_ref[0:1, :]
    sum_g = jnp.zeros((8, rows), F32)
    sum_gx = jnp.zeros((8, rows), F32)
    inv = jnp.zeros((8, rows), F32)
    for j in range(pieces):
        there = mj_ref[j].astype(F32) > 0.0

        def col(n):
            return e_ref[:, j * STATS + n : j * STATS + n + 1]

        share = jnp.exp(col(0) - log_total)
        g = jnp.where(there, share * col(3) - col(5), 0.0).reshape(pairs // 8, 8, rows)
        gx = jnp.where(there, share * col(4) - col(6), 0.0).reshape(pairs // 8, 8, rows)
        sum_g = sum_g + jnp.sum(g, axis=0)
        sum_gx = sum_gx + jnp.sum(gx, axis=0)
        inv = jnp.maximum(inv, jnp.max(jnp.where(there, col(2), 0.0).reshape(pairs // 8, 8, rows), axis=0))
    sub = lax.broadcasted_iota(I32, (8, rows), 0)
    sum_g = jnp.sum(sum_g, axis=0, keepdims=True)
    sum_gx = jnp.sum(sum_gx, axis=0, keepdims=True)
    inv = jnp.max(inv, axis=0, keepdims=True)
    out_ref[...] = jnp.where(sub == 0, sum_g, jnp.where(sub == 1, sum_gx, inv))


def final_kernel(r_ref, m_ref, c_ref, gain_ref, sums_ref, out_ref, *, total):
    grad = dot(m_ref[...], r_ref[...], 0, 0)
    rows = grad.shape[0]
    cols = jnp.concatenate(
        [jnp.transpose(sums_ref[:, c * 128 : (c + 1) * 128])[:, 0:3] for c in range(rows // 128)], axis=0
    )
    inv = cols[:, 2:3]
    g = grad * gain_ref[...]
    centered = c_ref[...] * inv
    out_ref[...] = inv * (g - cols[:, 0:1] / total - centered * (cols[:, 1:2] / total))


def step(
    queries,
    enc_keys,
    enc_values,
    source_lengths,
    out_proj,
    dec_state,
    norm_gain,
    norm_bias,
    head_weight,
    shortlist,
    target_slot,
    target_offset,
):
    vocs = lax.axis_size("vocab")
    chips = lax.axis_size("chip")
    places = ("chip", "vocab")
    rows, width = dec_state.shape
    mem = enc_keys.shape[1]
    total = out_proj.shape[1]
    blocks = head_weight.shape[1] // BLK
    group = -(-blocks // chips)
    tokens = group * BLK
    pieces = group * MOST
    pairs = chips * vocs
    slots = pairs * pieces
    span = vocs * pieces
    here = jnp.stack([lax.axis_index("chip"), lax.axis_index("core")]).astype(I32)
    gain = norm_gain.reshape(1, width)
    bias = norm_bias.reshape(1, width)
    partner = [(i, CORES - 1 - i) for i in range(CORES)]
    lists = shortlist.T

    def exchange(x, axis):
        return lax.all_to_all(x, axis, split_axis=0, concat_axis=0, tiled=True)

    (code,) = call(
        lambda *refs: code_kernel(*refs, blocks=blocks, group=group), [((span, 128), BF16)], [SM, VM, VM, VM]
    )(here, lists, target_slot.reshape(1, rows), target_offset.reshape(1, rows))
    codes = exchange(code.reshape(vocs, pieces, 128), "vocab").reshape(span, 128)
    (share,) = call(
        share_kernel, [((rows + 2 * mem + chips * width + EXTRA, width), BF16)], [SM] + [VM] * 5
    )(here, queries, enc_keys, enc_values, out_proj, dec_state)
    other = lax.ppermute(share, "core", partner)
    wsend = call(pack_kernel, [((width, tokens), BF16)] * chips, [SM, VM])(here, head_weight)
    win = [wsend[0]]
    for o in range(1, chips):
        win.append(lax.ppermute(wsend[o], "chip", [(i, (i + o) % chips) for i in range(chips)]))
    m, mj = call(
        lambda *refs: slots_kernel(*refs, blocks=blocks, group=group, vocs=vocs),
        [((slots, rows), BF16), ((pieces, pairs, rows), BF16)],
        [VM],
    )(lists)
    (parts,) = call(attend_kernel, [((chips, rows + EXTRA, width), BF16)], [SM, SM] + [VM] * 8)(
        here, source_lengths, queries, enc_keys, enc_values, out_proj, dec_state, gain, bias, other
    )
    parts = exchange(parts, "chip")
    c, extras, outgoing = call(
        lambda *refs: residual_kernel(*refs, total=total),
        [((rows, width), F32), ((chips, EXTRA, width), BF16), ((slots, width), BF16)],
        [VM] * 4,
    )(parts, dec_state, gain, m)
    incoming = exchange(outgoing.reshape(pairs, pieces, width), places)
    lines = 3 * (rows // 128)
    height = -(-(span + span // 128 + 2 * group) // 8) * 8
    (half,) = call(
        lambda *refs: half_kernel(*refs, group=group, lines=lines), [((height, BLK), F32)], [SM] + [VM] * (2 + chips)
    )(here, incoming.reshape(chips, span, width), extras, *win)
    half_in = lax.ppermute(half, "core", partner)
    logits, stats = call(
        lambda *refs: score_kernel(*refs, group=group, total=total),
        [((span, BLK), F32), ((pairs, 128), F32)],
        [VM] * 3,
        scratch=[pltpu.VMEM((span, BLK), F32)],
    )(half, half_in, codes)
    back_stats = exchange(stats.reshape(pairs, 1, 128), places).reshape(pairs, 128)
    totals, loss, back = call(
        total_kernel, [((8, rows), F32), ((1, rows), F32), ((span, 128), F32)], [SM, VM, VM, VM]
    )(here, back_stats, mj, m)
    back_in = exchange(back.reshape(vocs, pieces, 128), "vocab").reshape(span, 128)
    (grads,) = call(
        lambda *refs: delta_kernel(*refs, group=group), [((chips, span, width), BF16)], [SM] + [VM] * (3 + chips)
    )(here, logits, codes, back_in, *win)
    returned = exchange(grads.reshape(pairs, pieces, width), places).reshape(slots, width)
    (sums,) = call(sums_kernel, [((8, rows), F32)], [VM] * 3)(back_stats, mj, totals)
    (grad_state,) = call(
        lambda *refs: final_kernel(*refs, total=total), [((rows, width), F32)], [VM] * 5
    )(returned, m, c, gain, sums)
    return (loss.reshape(rows), grad_state)


def solution(mesh):
    src, vocs = mesh.devices.shape
    finer = Mesh(mesh.devices.reshape(src // CORES, CORES, vocs), ("chip", "core", "vocab"))
    feats = ("chip", "core")
    placed = (
        P("vocab", feats),
        P("vocab", None, feats),
        P("vocab", None, feats),
        P("vocab"),
        P(feats, None),
        P("vocab", feats),
        P(feats),
        P(feats),
        P(feats, "vocab"),
        P("vocab", None),
        P("vocab"),
        P("vocab"),
    )
    return jax.shard_map(
        step,
        mesh=finer,
        in_specs=placed,
        out_specs=(P("vocab"), P("vocab", feats)),
        check_vma=False,
    )
```

```python
import math

import jax
import jax.numpy as jnp
from jax import lax
from jax.experimental import pallas as pl
from jax.experimental.pallas import tpu as pltpu
from jax.sharding import Mesh
from jax.sharding import PartitionSpec as P


HD = 128
BLK = 128
MOST = 2
EPSILON = 1e-05
MASKED = -1e30
F32 = jnp.float32
BF16 = jnp.bfloat16
I32 = jnp.int32

VM = pl.BlockSpec(memory_space=pltpu.VMEM)
SM = pl.BlockSpec(memory_space=pltpu.SMEM)
CORES = 2
STATS = 8
EXTRA = 16


def call(body, outs, specs, scratch=()):
    return pl.pallas_call(
        body,
        out_shape=tuple(jax.ShapeDtypeStruct(s, d) for s, d in outs),
        in_specs=specs,
        out_specs=tuple(VM for _ in outs),
        scratch_shapes=list(scratch),
    )


def dot(a, b, ca, cb):
    return lax.dot_general(a, b, (((ca,), (cb,)), ((), ())), preferred_element_type=F32)


def thirds(x):
    hi = x.astype(BF16)
    rest = x - hi.astype(F32)
    mid = rest.astype(BF16)
    low = (rest - mid.astype(F32)).astype(BF16)
    return hi, mid, low


def stack_rows(lines, count, width):
    sub = lax.broadcasted_iota(I32, (count, width), 0)
    out = jnp.zeros((count, width), F32)
    for n, line in enumerate(lines):
        out = jnp.where(sub == n, line.astype(F32), out)
    return out


def pack_kernel(where_ref, head_ref, *out_refs):
    chips = len(out_refs)
    _, tokens = out_refs[0].shape
    cols = head_ref.shape[1]
    for o in range(chips):
        to = lax.rem(where_ref[0] + o, chips)
        start = pl.multiple_of(to * tokens, BLK)
        for t in range(tokens // BLK):
            first = start + t * BLK
            there = first < cols
            safe = pl.multiple_of(jnp.minimum(first, cols - BLK), BLK)
            piece = head_ref[:, pl.ds(safe, BLK)]
            out_refs[o][:, t * BLK : (t + 1) * BLK] = jnp.where(there, piece, jnp.zeros_like(piece))


def share_kernel(where_ref, q_ref, k_ref, v_ref, proj_ref, dec_ref, out_ref):
    rows, width = q_ref.shape
    mem = k_ref.shape[1]
    chips = proj_ref.shape[1] // (CORES * width)
    other = 1 - where_ref[1]
    out_ref[0:rows, :] = q_ref[...]
    out_ref[rows : rows + mem, :] = k_ref[0]
    out_ref[rows + mem : rows + 2 * mem, :] = v_ref[0]
    base = rows + 2 * mem
    for y in range(chips):
        cols = pl.ds(pl.multiple_of((y * CORES + other) * width, width), width)
        out_ref[base + y * width : base + (y + 1) * width, :] = proj_ref[:, cols]
    base = base + chips * width
    sums = dot(jnp.ones((8, proj_ref.shape[1]), BF16), proj_ref[...], 1, 1)
    dec_sums = dot(jnp.ones((8, width), BF16), dec_ref[...], 1, 1)
    lines = list(thirds(sums[0:1, :]))
    for third in thirds(dec_sums[0:1, :]):
        lines += [third[:, c * 128 : (c + 1) * 128] for c in range(rows // 128)]
    out_ref[base:, :] = stack_rows(lines, EXTRA, width).astype(BF16)


def mask_of(listed, earlier, u, v, j, blocks, group):
    local = u * group + lax.rem(j, group)
    block = jnp.where(local < blocks, v * blocks + local, -1)
    named = block == listed[0:1, :]
    for k in range(1, listed.shape[0]):
        named = jnp.logical_or(named, block == listed[k : k + 1, :])
    named = named.astype(F32)
    rank = dot(named.astype(BF16), earlier, 1, 0)
    return jnp.where(rank == lax.div(j, group).astype(F32), named, 0.0), block


def earlier_of(rows):
    r0 = lax.broadcasted_iota(I32, (rows, rows), 0)
    r1 = lax.broadcasted_iota(I32, (rows, rows), 1)
    return (r0 < r1).astype(F32).astype(BF16)


def code_kernel(where_ref, list_ref, tslot_ref, toff_ref, code_ref, *, blocks, group):
    pieces = group * MOST
    span = code_ref.shape[0]
    listed = list_ref[...]
    tslot = tslot_ref[...]
    rows = listed.shape[1]
    target_block = jnp.zeros((1, rows), I32)
    for k in range(listed.shape[0]):
        target_block = jnp.where(tslot == k, listed[k : k + 1, :], target_block)
    i = lax.broadcasted_iota(I32, (span, 1), 0)
    u = jnp.full((span, 1), where_ref[0], I32)
    m, block = mask_of(listed, earlier_of(rows), u, lax.div(i, pieces), lax.rem(i, pieces), blocks, group)
    hit = jnp.where(block == target_block, toff_ref[...].astype(F32) + 1.0, 0.0)
    code = jnp.sum(m * (hit + 1.0), axis=1, keepdims=True) - 2.0
    code_ref[...] = jnp.broadcast_to(code, code_ref.shape).astype(BF16)


def slots_kernel(list_ref, m_ref, *, blocks, group, vocs):
    pieces = group * MOST
    slots, rows = m_ref.shape
    listed = list_ref[...]
    earlier = earlier_of(rows)
    step = 256
    span = vocs * pieces
    sub = lax.broadcasted_iota(I32, (step, 1), 0)

    def travel(t, carry):
        i = t * step + sub
        u = lax.div(i, span)
        v = lax.div(lax.rem(i, span), pieces)
        m, _ = mask_of(listed, earlier, u, v, lax.rem(i, pieces), blocks, group)
        m_ref[pl.ds(pl.multiple_of(t * step, step), step), :] = m.astype(BF16)
        return carry

    lax.fori_loop(0, slots // step, travel, 0)


def major_kernel(list_ref, mj_ref, *, blocks, group, vocs):
    pieces, pairs, rows = mj_ref.shape
    listed = list_ref[...]
    earlier = earlier_of(rows)
    w = lax.broadcasted_iota(I32, (pairs, 1), 0)

    def major(t, carry):
        j = jnp.full((pairs, 1), t, I32)
        m, _ = mask_of(listed, earlier, lax.div(w, vocs), lax.rem(w, vocs), j, blocks, group)
        mj_ref[t] = m.astype(BF16)
        return carry

    lax.fori_loop(0, pieces, major, 0)


def whole_line(lines, first, n):
    cut = [lines[first + i : first + i + 1] for i in range(3 * n)]
    return jnp.concatenate([cut[c] + cut[n + c] + cut[2 * n + c] for c in range(n)], axis=1)


def attend(q, k, v, length):
    scores = dot(q, k, 1, 1) * (1.0 / math.sqrt(HD))
    usable = lax.broadcasted_iota(I32, scores.shape, 1) < length
    scores = jnp.where(usable, scores, MASKED)
    top = jnp.max(scores, axis=1, keepdims=True)
    raw = jnp.where(usable, jnp.exp(scores - top), 0.0)
    totals = jnp.sum(raw, axis=1, keepdims=True)
    return (dot(raw.astype(BF16), v, 1, 0) / totals).astype(BF16)


def attend_kernel(
    where_ref, len_ref, q_ref, k_ref, v_ref, proj_ref, dec_ref, gain_ref, bias_ref, other_ref, out_ref
):
    chips, _, width = out_ref.shape
    rows = q_ref.shape[0]
    mem = k_ref.shape[1]
    core = where_ref[1]
    length = len_ref[0]
    att = attend(q_ref[...], k_ref[0], v_ref[0], length)
    q2, k2, v2 = other_ref[0:rows, :], other_ref[rows : rows + mem, :], other_ref[rows + mem : rows + 2 * mem, :]
    att2 = attend(q2, k2, v2, length)
    base = rows + 2 * mem
    for y in range(chips):
        own = proj_ref[:, pl.ds(pl.multiple_of((y * CORES + core) * width, width), width)]
        out_ref[y, :rows, :] = (
            dot(att, own, 1, 0) + dot(att2, other_ref[base + y * width : base + (y + 1) * width, :], 1, 0)
        ).astype(BF16)
    base = base + chips * width
    sums = dot(jnp.ones((8, proj_ref.shape[1]), BF16), proj_ref[...], 1, 1)
    part = dot(jnp.ones((8, width), BF16), dec_ref[...], 1, 1)
    for third in thirds(sums):
        part = part + dot(third, att, 1, 1)
    other_sums = dot(other_ref[base:, :], att2, 1, 1)
    line = part[0:1, :] + (other_sums[0:1, :] + other_sums[1:2, :] + other_sums[2:3, :])
    line = line + whole_line(other_ref[base:, :].astype(F32), 3, rows // 128)
    lines = []
    for third in thirds(line):
        lines += [third[:, c * 128 : (c + 1) * 128] for c in range(rows // 128)]
    lines += list(thirds(gain_ref[...])) + list(thirds(bias_ref[...]))
    extra = stack_rows(lines, EXTRA, width).astype(BF16)
    for y in range(chips):
        out_ref[y, rows:, :] = extra


def columns(line):
    n = line.shape[1] // 128
    parts = [jnp.transpose(jnp.broadcast_to(line[:, c * 128 : (c + 1) * 128], (8, 128)))[:, 0:1] for c in range(n)]
    return jnp.concatenate(parts, axis=0)


def residual_kernel(part_ref, dec_ref, gain_ref, m_ref, c_ref, extra_ref, out_ref, *, total):
    chips, _, width = part_ref.shape
    rows = dec_ref.shape[0]
    acc = dec_ref[...].astype(F32)
    lines = jnp.zeros((EXTRA, width), F32)
    for y in range(chips):
        acc = acc + part_ref[y, :rows, :].astype(F32)
        lines = lines + part_ref[y, rows:, :].astype(F32)
        extra_ref[y] = part_ref[y, rows:, :]
    line = whole_line(lines, 0, rows // 128)
    c = acc - columns(line) / total
    c_ref[...] = c
    x = (c * gain_ref[...]).astype(BF16)
    out_ref[...] = dot(m_ref[...], x, 1, 0).astype(BF16)


def third_sum(x, first):
    return x[first : first + 1] + x[first + 1 : first + 2] + x[first + 2 : first + 3]


def half_kernel(where_ref, x_ref, extra_ref, *refs, group, lines):
    w_refs, out_ref = refs[:-1], refs[-1]
    chips, slots, width = x_ref.shape
    tokens = group * BLK
    acc = jnp.zeros((slots, tokens), F32)
    sums = jnp.zeros((EXTRA, tokens), F32)
    squares = jnp.zeros((slots, width), F32)
    for o in range(chips):
        y = lax.rem(where_ref[0] + (chips - o), chips)
        x = x_ref[y]
        w = w_refs[o][...]
        acc = acc + dot(x, w, 1, 0)
        small = extra_ref[y]
        plain = x.astype(F32) / third_sum(small.astype(F32), lines)
        squares = squares + plain * plain
        sums = sums + dot(small, w, 1, 0)
    place = lax.rem(lax.broadcasted_iota(I32, (slots, 1), 0), group)
    dots = acc[:, 0:BLK]
    for b in range(1, group):
        dots = jnp.where(place == b, acc[:, b * BLK : (b + 1) * BLK], dots)
    out_ref[0:slots, :] = dots
    ones = jnp.ones((8, width), BF16)
    total = jnp.zeros((8, slots), F32)
    for third in thirds(squares):
        total = total + dot(ones, third, 1, 1)
    base = slots
    n = slots // 128
    for c in range(n):
        out_ref[base + c : base + c + 1, :] = total[0:1, c * 128 : (c + 1) * 128]
    base = base + n
    for first in (lines, lines + 3):
        line = third_sum(sums, first)
        for b in range(group):
            out_ref[base + b : base + b + 1, :] = line[:, b * BLK : (b + 1) * BLK]
        base = base + group
    if base < out_ref.shape[0]:
        out_ref[base:, :] = jnp.zeros((out_ref.shape[0] - base, BLK), F32)


def score_kernel(own_ref, other_ref, code_ref, l_ref, row_ref, stat_ref, *, group, total):
    slots = l_ref.shape[0]
    pieces = MOST * group
    both = own_ref[...] + other_ref[...]
    dots = both[0:slots]
    n = slots // 128
    squares = columns(jnp.concatenate([both[slots + c : slots + c + 1] for c in range(n)], axis=1))
    inv = lax.rsqrt(squares / total + EPSILON)
    place = lax.rem(lax.broadcasted_iota(I32, (slots, 1), 0), group)
    at = slots + n
    gains = jnp.broadcast_to(both[at : at + 1], dots.shape)
    biases = jnp.broadcast_to(both[at + group : at + group + 1], dots.shape)
    for b in range(1, group):
        gains = jnp.where(place == b, both[at + b : at + b + 1], gains)
        biases = jnp.where(place == b, both[at + group + b : at + group + b + 1], biases)
    bare = inv * dots
    logits = bare + biases
    l_ref[...] = logits
    top = jnp.max(logits, axis=1, keepdims=True)
    shifted = jnp.exp(logits - top)
    spread = jnp.sum(shifted, axis=1, keepdims=True)
    lse = top + jnp.log(spread)
    soft = shifted / spread
    lane = lax.broadcasted_iota(I32, logits.shape, 1)
    hit = lane.astype(F32) == code_ref[...].astype(F32)

    def row_sum(v):
        return jnp.sum(v, axis=1, keepdims=True)

    cols = [
        lse,
        row_sum(jnp.where(hit, logits, 0.0)),
        inv,
        row_sum(soft * gains),
        row_sum(soft * bare),
        row_sum(jnp.where(hit, gains, 0.0)),
        row_sum(jnp.where(hit, bare, 0.0)),
    ]
    out = jnp.zeros(logits.shape, F32)
    for n, col in enumerate(cols):
        out = jnp.where(lane == n, col, out)
    stat_ref[...] = out
    sents = slots // pieces
    lane_s = lax.div(lax.broadcasted_iota(I32, (sents, 128), 1), STATS)
    packed = jnp.zeros((sents, 128), F32)
    for j in range(pieces):
        z = stat_ref[pl.ds(j, sents, stride=pieces), :]
        if j:
            z = pltpu.roll(z, j * STATS, 1)
        packed = jnp.where(lane_s == j, z, packed)
    for u in range(row_ref.shape[0] // sents):
        row_ref[u * sents : (u + 1) * sents, :] = packed


def total_kernel(where_ref, e_ref, mj_ref, m_ref, tot_ref, loss_ref, back_ref):
    pieces, pairs, rows = mj_ref.shape
    low = jnp.full((8, rows), MASKED, F32)
    for j in range(pieces):
        lse = jnp.where(mj_ref[j].astype(F32) > 0.0, e_ref[:, j * STATS : j * STATS + 1], MASKED)
        low = jnp.maximum(low, jnp.max(lse.reshape(pairs // 8, 8, rows), axis=0))
    low = jnp.max(low, axis=0, keepdims=True)
    total = jnp.zeros((8, rows), F32)
    picked = jnp.zeros((8, rows), F32)
    for j in range(pieces):
        there = mj_ref[j].astype(F32) > 0.0
        lse = e_ref[:, j * STATS : j * STATS + 1]
        pick = e_ref[:, j * STATS + 1 : j * STATS + 2]
        total = total + jnp.sum(jnp.where(there, jnp.exp(lse - low), 0.0).reshape(pairs // 8, 8, rows), axis=0)
        picked = picked + jnp.sum(jnp.where(there, pick, 0.0).reshape(pairs // 8, 8, rows), axis=0)
    log_total = low + jnp.log(jnp.sum(total, axis=0, keepdims=True))
    tot_ref[...] = jnp.broadcast_to(log_total, tot_ref.shape)
    loss_ref[...] = log_total - jnp.sum(picked, axis=0, keepdims=True)
    slots = back_ref.shape[0]
    own = m_ref[pl.ds(pl.multiple_of(where_ref[0] * slots, slots), slots), :].astype(F32)
    back_ref[...] = jnp.broadcast_to(jnp.sum(own * log_total, axis=1, keepdims=True), back_ref.shape)


def delta_kernel(where_ref, l_ref, code_ref, back_ref, *refs, group):
    w_refs, out_ref = refs[:-1], refs[-1]
    chips = len(w_refs)
    logits = l_ref[...]
    code = code_ref[...].astype(F32)
    lane = lax.broadcasted_iota(I32, logits.shape, 1).astype(F32)
    deltas = jnp.exp(logits - back_ref[...]) - jnp.where(lane == code, 1.0, 0.0)
    deltas = jnp.where(code > -1.5, deltas, 0.0)
    place = lax.rem(lax.broadcasted_iota(I32, logits.shape, 0), group)
    wide = jnp.concatenate([jnp.where(place == b, deltas, 0.0).astype(BF16) for b in range(group)], axis=1)
    for o in range(chips):
        y = lax.rem(where_ref[0] + (chips - o), chips)
        out_ref[y] = dot(wide, w_refs[o][...], 1, 1).astype(BF16)


def sums_kernel(e_ref, mj_ref, tot_ref, out_ref):
    pieces, pairs, rows = mj_ref.shape
    log_total = tot_ref[0:1, :]
    sum_g = jnp.zeros((8, rows), F32)
    sum_gx = jnp.zeros((8, rows), F32)
    inv = jnp.zeros((8, rows), F32)
    for j in range(pieces):
        there = mj_ref[j].astype(F32) > 0.0

        def col(n):
            return e_ref[:, j * STATS + n : j * STATS + n + 1]

        share = jnp.exp(col(0) - log_total)
        g = jnp.where(there, share * col(3) - col(5), 0.0).reshape(pairs // 8, 8, rows)
        gx = jnp.where(there, share * col(4) - col(6), 0.0).reshape(pairs // 8, 8, rows)
        sum_g = sum_g + jnp.sum(g, axis=0)
        sum_gx = sum_gx + jnp.sum(gx, axis=0)
        inv = jnp.maximum(inv, jnp.max(jnp.where(there, col(2), 0.0).reshape(pairs // 8, 8, rows), axis=0))
    sub = lax.broadcasted_iota(I32, (8, rows), 0)
    sum_g = jnp.sum(sum_g, axis=0, keepdims=True)
    sum_gx = jnp.sum(sum_gx, axis=0, keepdims=True)
    inv = jnp.max(inv, axis=0, keepdims=True)
    out_ref[...] = jnp.where(sub == 0, sum_g, jnp.where(sub == 1, sum_gx, inv))


def final_kernel(r_ref, m_ref, c_ref, gain_ref, sums_ref, out_ref, *, total):
    grad = dot(m_ref[...], r_ref[...], 0, 0)
    rows = grad.shape[0]
    cols = jnp.concatenate(
        [jnp.transpose(sums_ref[:, c * 128 : (c + 1) * 128])[:, 0:3] for c in range(rows // 128)], axis=0
    )
    inv = cols[:, 2:3]
    g = grad * gain_ref[...]
    centered = c_ref[...] * inv
    out_ref[...] = inv * (g - cols[:, 0:1] / total - centered * (cols[:, 1:2] / total))


def step(
    queries,
    enc_keys,
    enc_values,
    source_lengths,
    out_proj,
    dec_state,
    norm_gain,
    norm_bias,
    head_weight,
    shortlist,
    target_slot,
    target_offset,
):
    vocs = lax.axis_size("vocab")
    chips = lax.axis_size("chip")
    places = ("chip", "vocab")
    rows, width = dec_state.shape
    mem = enc_keys.shape[1]
    total = out_proj.shape[1]
    blocks = head_weight.shape[1] // BLK
    group = -(-blocks // chips)
    tokens = group * BLK
    pieces = group * MOST
    pairs = chips * vocs
    slots = pairs * pieces
    span = vocs * pieces
    here = jnp.stack([lax.axis_index("chip"), lax.axis_index("core")]).astype(I32)
    gain = norm_gain.reshape(1, width)
    bias = norm_bias.reshape(1, width)
    partner = [(i, CORES - 1 - i) for i in range(CORES)]
    lists = shortlist.T

    def exchange(x, axis):
        return lax.all_to_all(x, axis, split_axis=0, concat_axis=0, tiled=True)

    (code,) = call(
        lambda *refs: code_kernel(*refs, blocks=blocks, group=group), [((span, 128), BF16)], [SM, VM, VM, VM]
    )(here, lists, target_slot.reshape(1, rows), target_offset.reshape(1, rows))
    codes = exchange(code.reshape(vocs, pieces, 128), "vocab").reshape(span, 128)
    (share,) = call(
        share_kernel, [((rows + 2 * mem + chips * width + EXTRA, width), BF16)], [SM] + [VM] * 5
    )(here, queries, enc_keys, enc_values, out_proj, dec_state)
    other = lax.ppermute(share, "core", partner)
    wsend = call(pack_kernel, [((width, tokens), BF16)] * chips, [SM, VM])(here, head_weight)
    win = [wsend[0]]
    for o in range(1, chips):
        win.append(lax.ppermute(wsend[o], "chip", [(i, (i + o) % chips) for i in range(chips)]))
    (m,) = call(
        lambda *refs: slots_kernel(*refs, blocks=blocks, group=group, vocs=vocs), [((slots, rows), BF16)], [VM]
    )(lists)
    (mj,) = call(
        lambda *refs: major_kernel(*refs, blocks=blocks, group=group, vocs=vocs), [((pieces, pairs, rows), BF16)], [VM]
    )(lists)
    (parts,) = call(attend_kernel, [((chips, rows + EXTRA, width), BF16)], [SM, SM] + [VM] * 8)(
        here, source_lengths, queries, enc_keys, enc_values, out_proj, dec_state, gain, bias, other
    )
    parts = exchange(parts, "chip")
    c, extras, outgoing = call(
        lambda *refs: residual_kernel(*refs, total=total),
        [((rows, width), F32), ((chips, EXTRA, width), BF16), ((slots, width), BF16)],
        [VM] * 4,
    )(parts, dec_state, gain, m)
    incoming = exchange(outgoing.reshape(pairs, pieces, width), places)
    lines = 3 * (rows // 128)
    height = -(-(span + span // 128 + 2 * group) // 8) * 8
    (half,) = call(
        lambda *refs: half_kernel(*refs, group=group, lines=lines), [((height, BLK), F32)], [SM] + [VM] * (2 + chips)
    )(here, incoming.reshape(chips, span, width), extras, *win)
    half_in = lax.ppermute(half, "core", partner)
    logits, stats = call(
        lambda *refs: score_kernel(*refs, group=group, total=total),
        [((span, BLK), F32), ((pairs, 128), F32)],
        [VM] * 3,
        scratch=[pltpu.VMEM((span, BLK), F32)],
    )(half, half_in, codes)
    back_stats = exchange(stats.reshape(pairs, 1, 128), places).reshape(pairs, 128)
    totals, loss, back = call(
        total_kernel, [((8, rows), F32), ((1, rows), F32), ((span, 128), F32)], [SM, VM, VM, VM]
    )(here, back_stats, mj, m)
    back_in = exchange(back.reshape(vocs, pieces, 128), "vocab").reshape(span, 128)
    (grads,) = call(
        lambda *refs: delta_kernel(*refs, group=group), [((chips, span, width), BF16)], [SM] + [VM] * (3 + chips)
    )(here, logits, codes, back_in, *win)
    returned = exchange(grads.reshape(pairs, pieces, width), places).reshape(slots, width)
    (sums,) = call(sums_kernel, [((8, rows), F32)], [VM] * 3)(back_stats, mj, totals)
    (grad_state,) = call(
        lambda *refs: final_kernel(*refs, total=total), [((rows, width), F32)], [VM] * 5
    )(returned, m, c, gain, sums)
    return (loss.reshape(rows), grad_state)


def solution(mesh):
    src, vocs = mesh.devices.shape
    finer = Mesh(mesh.devices.reshape(src // CORES, CORES, vocs), ("chip", "core", "vocab"))
    feats = ("chip", "core")
    placed = (
        P("vocab", feats),
        P("vocab", None, feats),
        P("vocab", None, feats),
        P("vocab"),
        P(feats, None),
        P("vocab", feats),
        P(feats),
        P(feats),
        P(feats, "vocab"),
        P("vocab", None),
        P("vocab"),
        P("vocab"),
    )
    return jax.shard_map(
        step,
        mesh=finer,
        in_specs=placed,
        out_specs=(P("vocab"), P("vocab", feats)),
        check_vma=False,
    )
```

```python
import math

import jax
import jax.numpy as jnp
from jax import lax
from jax.experimental import pallas as pl
from jax.experimental.pallas import tpu as pltpu
from jax.sharding import Mesh
from jax.sharding import PartitionSpec as P


HD = 128
BLK = 128
MOST = 2
EPSILON = 1e-05
MASKED = -1e30
F32 = jnp.float32
BF16 = jnp.bfloat16
I32 = jnp.int32

VM = pl.BlockSpec(memory_space=pltpu.VMEM)
SM = pl.BlockSpec(memory_space=pltpu.SMEM)
CORES = 2
STATS = 8
EXTRA = 16


def call(body, outs, specs, scratch=()):
    return pl.pallas_call(
        body,
        out_shape=tuple(jax.ShapeDtypeStruct(s, d) for s, d in outs),
        in_specs=specs,
        out_specs=tuple(VM for _ in outs),
        scratch_shapes=list(scratch),
    )


def dot(a, b, ca, cb):
    return lax.dot_general(a, b, (((ca,), (cb,)), ((), ())), preferred_element_type=F32)


def thirds(x):
    hi = x.astype(BF16)
    rest = x - hi.astype(F32)
    mid = rest.astype(BF16)
    low = (rest - mid.astype(F32)).astype(BF16)
    return hi, mid, low


def stack_rows(lines, count, width):
    sub = lax.broadcasted_iota(I32, (count, width), 0)
    out = jnp.zeros((count, width), F32)
    for n, line in enumerate(lines):
        out = jnp.where(sub == n, line.astype(F32), out)
    return out


def pack_kernel(where_ref, head_ref, *out_refs):
    chips = len(out_refs)
    _, tokens = out_refs[0].shape
    cols = head_ref.shape[1]
    for o in range(chips):
        to = lax.rem(where_ref[0] + o, chips)
        start = pl.multiple_of(to * tokens, BLK)
        for t in range(tokens // BLK):
            first = start + t * BLK
            there = first < cols
            safe = pl.multiple_of(jnp.minimum(first, cols - BLK), BLK)
            piece = head_ref[:, pl.ds(safe, BLK)]
            out_refs[o][:, t * BLK : (t + 1) * BLK] = jnp.where(there, piece, jnp.zeros_like(piece))


def share_kernel(where_ref, q_ref, k_ref, v_ref, proj_ref, dec_ref, out_ref):
    rows, width = q_ref.shape
    mem = k_ref.shape[1]
    chips = proj_ref.shape[1] // (CORES * width)
    other = 1 - where_ref[1]
    out_ref[0:rows, :] = q_ref[...]
    out_ref[rows : rows + mem, :] = k_ref[0]
    out_ref[rows + mem : rows + 2 * mem, :] = v_ref[0]
    base = rows + 2 * mem
    for y in range(chips):
        cols = pl.ds(pl.multiple_of((y * CORES + other) * width, width), width)
        out_ref[base + y * width : base + (y + 1) * width, :] = proj_ref[:, cols]
    base = base + chips * width
    sums = dot(jnp.ones((8, proj_ref.shape[1]), BF16), proj_ref[...], 1, 1)
    dec_sums = dot(jnp.ones((8, width), BF16), dec_ref[...], 1, 1)
    lines = list(thirds(sums[0:1, :]))
    for third in thirds(dec_sums[0:1, :]):
        lines += [third[:, c * 128 : (c + 1) * 128] for c in range(rows // 128)]
    out_ref[base:, :] = stack_rows(lines, EXTRA, width).astype(BF16)


def mask_of(listed, earlier, u, v, j, blocks, group):
    local = u * group + lax.rem(j, group)
    block = jnp.where(local < blocks, v * blocks + local, -1)
    named = block == listed[0:1, :]
    for k in range(1, listed.shape[0]):
        named = jnp.logical_or(named, block == listed[k : k + 1, :])
    named = named.astype(F32)
    rank = dot(named.astype(BF16), earlier, 1, 0)
    return jnp.where(rank == lax.div(j, group).astype(F32), named, 0.0), block


def earlier_of(rows):
    r0 = lax.broadcasted_iota(I32, (rows, rows), 0)
    r1 = lax.broadcasted_iota(I32, (rows, rows), 1)
    return (r0 < r1).astype(F32).astype(BF16)


def code_kernel(where_ref, all_ref, code_ref, named_ref, value_ref, *, blocks, group, picks):
    sents, _, rows = all_ref.shape
    pieces = group * MOST
    j = lax.broadcasted_iota(I32, (pieces, 1), 0)
    local = where_ref[0] * group + lax.rem(j, group)
    block = jnp.where(local < blocks, where_ref[2] * blocks + local, -1)

    def sentence(t, carry):
        listed = all_ref[t]
        named = block == listed[0:1, :]
        tslot = listed[picks : picks + 1, :]
        target_block = jnp.where(tslot == 0, listed[0:1, :], 0)
        for k in range(1, picks):
            named = jnp.logical_or(named, block == listed[k : k + 1, :])
            target_block = jnp.where(tslot == k, listed[k : k + 1, :], target_block)
        hit = jnp.where(block == target_block, listed[picks + 1 : picks + 2, :] + 2, 1).astype(F32)
        at = pl.ds(pl.multiple_of(t * pieces, pieces), pieces)
        named_ref[at, :] = named.astype(F32)
        value_ref[at, :] = jnp.where(named, hit, 0.0)
        return carry

    lax.fori_loop(0, sents, sentence, 0)
    rank = dot(named_ref[...].astype(BF16), earlier_of(rows), 1, 0)
    place = lax.rem(lax.broadcasted_iota(I32, (sents * pieces, 1), 0), pieces)
    want = lax.div(place, group).astype(F32)
    code = jnp.sum(jnp.where(rank == want, value_ref[...], 0.0), axis=1, keepdims=True) - 2.0
    code_ref[...] = jnp.broadcast_to(code, code_ref.shape)


def slots_kernel(list_ref, m_ref, *, blocks, group, vocs):
    pieces = group * MOST
    slots, rows = m_ref.shape
    listed = list_ref[...]
    earlier = earlier_of(rows)
    step = 256
    span = vocs * pieces
    sub = lax.broadcasted_iota(I32, (step, 1), 0)

    def travel(t, carry):
        i = t * step + sub
        u = lax.div(i, span)
        v = lax.div(lax.rem(i, span), pieces)
        m, _ = mask_of(listed, earlier, u, v, lax.rem(i, pieces), blocks, group)
        m_ref[pl.ds(pl.multiple_of(t * step, step), step), :] = m.astype(BF16)
        return carry

    lax.fori_loop(0, slots // step, travel, 0)


def major_kernel(list_ref, mj_ref, *, blocks, group, vocs):
    pieces, pairs, rows = mj_ref.shape
    listed = list_ref[...]
    earlier = earlier_of(rows)
    w = lax.broadcasted_iota(I32, (pairs, 1), 0)

    def major(t, carry):
        j = jnp.full((pairs, 1), t, I32)
        m, _ = mask_of(listed, earlier, lax.div(w, vocs), lax.rem(w, vocs), j, blocks, group)
        mj_ref[t] = m.astype(BF16)
        return carry

    lax.fori_loop(0, pieces, major, 0)


def whole_line(lines, first, n):
    cut = [lines[first + i : first + i + 1] for i in range(3 * n)]
    return jnp.concatenate([cut[c] + cut[n + c] + cut[2 * n + c] for c in range(n)], axis=1)


def attend(q, k, v, length):
    scores = dot(q, k, 1, 1) * (1.0 / math.sqrt(HD))
    usable = lax.broadcasted_iota(I32, scores.shape, 1) < length
    scores = jnp.where(usable, scores, MASKED)
    top = jnp.max(scores, axis=1, keepdims=True)
    raw = jnp.where(usable, jnp.exp(scores - top), 0.0)
    totals = jnp.sum(raw, axis=1, keepdims=True)
    return (dot(raw.astype(BF16), v, 1, 0) / totals).astype(BF16)


def attend_kernel(
    where_ref, len_ref, q_ref, k_ref, v_ref, proj_ref, dec_ref, gain_ref, bias_ref, other_ref, out_ref
):
    chips, _, width = out_ref.shape
    rows = q_ref.shape[0]
    mem = k_ref.shape[1]
    core = where_ref[1]
    length = len_ref[0]
    att = attend(q_ref[...], k_ref[0], v_ref[0], length)
    q2, k2, v2 = other_ref[0:rows, :], other_ref[rows : rows + mem, :], other_ref[rows + mem : rows + 2 * mem, :]
    att2 = attend(q2, k2, v2, length)
    base = rows + 2 * mem
    for y in range(chips):
        own = proj_ref[:, pl.ds(pl.multiple_of((y * CORES + core) * width, width), width)]
        out_ref[y, :rows, :] = (
            dot(att, own, 1, 0) + dot(att2, other_ref[base + y * width : base + (y + 1) * width, :], 1, 0)
        ).astype(BF16)
    base = base + chips * width
    sums = dot(jnp.ones((8, proj_ref.shape[1]), BF16), proj_ref[...], 1, 1)
    part = dot(jnp.ones((8, width), BF16), dec_ref[...], 1, 1)
    for third in thirds(sums):
        part = part + dot(third, att, 1, 1)
    other_sums = dot(other_ref[base:, :], att2, 1, 1)
    line = part[0:1, :] + (other_sums[0:1, :] + other_sums[1:2, :] + other_sums[2:3, :])
    line = line + whole_line(other_ref[base:, :].astype(F32), 3, rows // 128)
    lines = []
    for third in thirds(line):
        lines += [third[:, c * 128 : (c + 1) * 128] for c in range(rows // 128)]
    lines += list(thirds(gain_ref[...])) + list(thirds(bias_ref[...]))
    extra = stack_rows(lines, EXTRA, width).astype(BF16)
    for y in range(chips):
        out_ref[y, rows:, :] = extra


def columns(line):
    n = line.shape[1] // 128
    parts = [jnp.transpose(jnp.broadcast_to(line[:, c * 128 : (c + 1) * 128], (8, 128)))[:, 0:1] for c in range(n)]
    return jnp.concatenate(parts, axis=0)


def residual_kernel(part_ref, dec_ref, gain_ref, m_ref, c_ref, extra_ref, out_ref, *, total):
    chips, _, width = part_ref.shape
    rows = dec_ref.shape[0]
    acc = dec_ref[...].astype(F32)
    lines = jnp.zeros((EXTRA, width), F32)
    for y in range(chips):
        acc = acc + part_ref[y, :rows, :].astype(F32)
        lines = lines + part_ref[y, rows:, :].astype(F32)
        extra_ref[y] = part_ref[y, rows:, :]
    line = whole_line(lines, 0, rows // 128)
    c = acc - columns(line) / total
    c_ref[...] = c
    x = (c * gain_ref[...]).astype(BF16)
    out_ref[...] = dot(m_ref[...], x, 1, 0).astype(BF16)


def third_sum(x, first):
    return x[first : first + 1] + x[first + 1 : first + 2] + x[first + 2 : first + 3]


def half_kernel(where_ref, x_ref, extra_ref, *refs, group, lines):
    w_refs, out_ref = refs[:-1], refs[-1]
    chips, slots, width = x_ref.shape
    tokens = group * BLK
    acc = jnp.zeros((slots, tokens), F32)
    sums = jnp.zeros((EXTRA, tokens), F32)
    squares = jnp.zeros((slots, width), F32)
    for o in range(chips):
        y = lax.rem(where_ref[0] + (chips - o), chips)
        x = x_ref[y]
        w = w_refs[o][...]
        acc = acc + dot(x, w, 1, 0)
        small = extra_ref[y]
        plain = x.astype(F32) / third_sum(small.astype(F32), lines)
        squares = squares + plain * plain
        sums = sums + dot(small, w, 1, 0)
    place = lax.rem(lax.broadcasted_iota(I32, (slots, 1), 0), group)
    dots = acc[:, 0:BLK]
    for b in range(1, group):
        dots = jnp.where(place == b, acc[:, b * BLK : (b + 1) * BLK], dots)
    out_ref[0:slots, :] = dots
    ones = jnp.ones((8, width), BF16)
    total = jnp.zeros((8, slots), F32)
    for third in thirds(squares):
        total = total + dot(ones, third, 1, 1)
    base = slots
    n = slots // 128
    for c in range(n):
        out_ref[base + c : base + c + 1, :] = total[0:1, c * 128 : (c + 1) * 128]
    base = base + n
    for first in (lines, lines + 3):
        line = third_sum(sums, first)
        for b in range(group):
            out_ref[base + b : base + b + 1, :] = line[:, b * BLK : (b + 1) * BLK]
        base = base + group
    if base < out_ref.shape[0]:
        out_ref[base:, :] = jnp.zeros((out_ref.shape[0] - base, BLK), F32)


def score_kernel(own_ref, other_ref, code_ref, l_ref, row_ref, stat_ref, *, group, total):
    slots = l_ref.shape[0]
    pieces = MOST * group
    both = own_ref[...] + other_ref[...]
    dots = both[0:slots]
    n = slots // 128
    squares = columns(jnp.concatenate([both[slots + c : slots + c + 1] for c in range(n)], axis=1))
    inv = lax.rsqrt(squares / total + EPSILON)
    place = lax.rem(lax.broadcasted_iota(I32, (slots, 1), 0), group)
    at = slots + n
    gains = jnp.broadcast_to(both[at : at + 1], dots.shape)
    biases = jnp.broadcast_to(both[at + group : at + group + 1], dots.shape)
    for b in range(1, group):
        gains = jnp.where(place == b, both[at + b : at + b + 1], gains)
        biases = jnp.where(place == b, both[at + group + b : at + group + b + 1], biases)
    bare = inv * dots
    logits = bare + biases
    l_ref[...] = logits
    top = jnp.max(logits, axis=1, keepdims=True)
    shifted = jnp.exp(logits - top)
    spread = jnp.sum(shifted, axis=1, keepdims=True)
    lse = top + jnp.log(spread)
    soft = shifted / spread
    lane = lax.broadcasted_iota(I32, logits.shape, 1)
    hit = lane.astype(F32) == code_ref[...].astype(F32)

    def row_sum(v):
        return jnp.sum(v, axis=1, keepdims=True)

    cols = [
        lse,
        row_sum(jnp.where(hit, logits, 0.0)),
        inv,
        row_sum(soft * gains),
        row_sum(soft * bare),
        row_sum(jnp.where(hit, gains, 0.0)),
        row_sum(jnp.where(hit, bare, 0.0)),
    ]
    out = jnp.zeros(logits.shape, F32)
    for n, col in enumerate(cols):
        out = jnp.where(lane == n, col, out)
    stat_ref[...] = out
    sents = slots // pieces
    lane_s = lax.div(lax.broadcasted_iota(I32, (sents, 128), 1), STATS)
    packed = jnp.zeros((sents, 128), F32)
    for j in range(pieces):
        z = stat_ref[pl.ds(j, sents, stride=pieces), :]
        if j:
            z = pltpu.roll(z, j * STATS, 1)
        packed = jnp.where(lane_s == j, z, packed)
    for u in range(row_ref.shape[0] // sents):
        row_ref[u * sents : (u + 1) * sents, :] = packed


def total_kernel(where_ref, e_ref, mj_ref, m_ref, tot_ref, loss_ref, back_ref):
    pieces, pairs, rows = mj_ref.shape
    low = jnp.full((8, rows), MASKED, F32)
    for j in range(pieces):
        lse = jnp.where(mj_ref[j].astype(F32) > 0.0, e_ref[:, j * STATS : j * STATS + 1], MASKED)
        low = jnp.maximum(low, jnp.max(lse.reshape(pairs // 8, 8, rows), axis=0))
    low = jnp.max(low, axis=0, keepdims=True)
    total = jnp.zeros((8, rows), F32)
    picked = jnp.zeros((8, rows), F32)
    for j in range(pieces):
        there = mj_ref[j].astype(F32) > 0.0
        lse = e_ref[:, j * STATS : j * STATS + 1]
        pick = e_ref[:, j * STATS + 1 : j * STATS + 2]
        total = total + jnp.sum(jnp.where(there, jnp.exp(lse - low), 0.0).reshape(pairs // 8, 8, rows), axis=0)
        picked = picked + jnp.sum(jnp.where(there, pick, 0.0).reshape(pairs // 8, 8, rows), axis=0)
    log_total = low + jnp.log(jnp.sum(total, axis=0, keepdims=True))
    tot_ref[...] = jnp.broadcast_to(log_total, tot_ref.shape)
    loss_ref[...] = log_total - jnp.sum(picked, axis=0, keepdims=True)
    slots = back_ref.shape[0]
    own = m_ref[pl.ds(pl.multiple_of(where_ref[0] * slots, slots), slots), :].astype(F32)
    back_ref[...] = jnp.broadcast_to(jnp.sum(own * log_total, axis=1, keepdims=True), back_ref.shape)


def delta_kernel(where_ref, l_ref, code_ref, back_ref, *refs, group):
    w_refs, out_ref = refs[:-1], refs[-1]
    chips = len(w_refs)
    logits = l_ref[...]
    code = code_ref[...].astype(F32)
    lane = lax.broadcasted_iota(I32, logits.shape, 1).astype(F32)
    deltas = jnp.exp(logits - back_ref[...]) - jnp.where(lane == code, 1.0, 0.0)
    deltas = jnp.where(code > -1.5, deltas, 0.0)
    place = lax.rem(lax.broadcasted_iota(I32, logits.shape, 0), group)
    wide = jnp.concatenate([jnp.where(place == b, deltas, 0.0).astype(BF16) for b in range(group)], axis=1)
    for o in range(chips):
        y = lax.rem(where_ref[0] + (chips - o), chips)
        out_ref[y] = dot(wide, w_refs[o][...], 1, 1).astype(BF16)


def sums_kernel(e_ref, mj_ref, tot_ref, out_ref):
    pieces, pairs, rows = mj_ref.shape
    log_total = tot_ref[0:1, :]
    sum_g = jnp.zeros((8, rows), F32)
    sum_gx = jnp.zeros((8, rows), F32)
    inv = jnp.zeros((8, rows), F32)
    for j in range(pieces):
        there = mj_ref[j].astype(F32) > 0.0

        def col(n):
            return e_ref[:, j * STATS + n : j * STATS + n + 1]

        share = jnp.exp(col(0) - log_total)
        g = jnp.where(there, share * col(3) - col(5), 0.0).reshape(pairs // 8, 8, rows)
        gx = jnp.where(there, share * col(4) - col(6), 0.0).reshape(pairs // 8, 8, rows)
        sum_g = sum_g + jnp.sum(g, axis=0)
        sum_gx = sum_gx + jnp.sum(gx, axis=0)
        inv = jnp.maximum(inv, jnp.max(jnp.where(there, col(2), 0.0).reshape(pairs // 8, 8, rows), axis=0))
    sub = lax.broadcasted_iota(I32, (8, rows), 0)
    sum_g = jnp.sum(sum_g, axis=0, keepdims=True)
    sum_gx = jnp.sum(sum_gx, axis=0, keepdims=True)
    inv = jnp.max(inv, axis=0, keepdims=True)
    out_ref[...] = jnp.where(sub == 0, sum_g, jnp.where(sub == 1, sum_gx, inv))


def final_kernel(r_ref, m_ref, c_ref, gain_ref, sums_ref, out_ref, *, total):
    grad = dot(m_ref[...], r_ref[...], 0, 0)
    rows = grad.shape[0]
    cols = jnp.concatenate(
        [jnp.transpose(sums_ref[:, c * 128 : (c + 1) * 128])[:, 0:3] for c in range(rows // 128)], axis=0
    )
    inv = cols[:, 2:3]
    g = grad * gain_ref[...]
    centered = c_ref[...] * inv
    out_ref[...] = inv * (g - cols[:, 0:1] / total - centered * (cols[:, 1:2] / total))


def step(
    queries,
    enc_keys,
    enc_values,
    source_lengths,
    out_proj,
    dec_state,
    norm_gain,
    norm_bias,
    head_weight,
    shortlist,
    target_slot,
    target_offset,
):
    vocs = lax.axis_size("vocab")
    chips = lax.axis_size("chip")
    places = ("chip", "vocab")
    rows, width = dec_state.shape
    mem = enc_keys.shape[1]
    total = out_proj.shape[1]
    blocks = head_weight.shape[1] // BLK
    group = -(-blocks // chips)
    tokens = group * BLK
    pieces = group * MOST
    pairs = chips * vocs
    slots = pairs * pieces
    span = vocs * pieces
    here = jnp.stack([lax.axis_index("chip"), lax.axis_index("core"), lax.axis_index("vocab")]).astype(I32)
    gain = norm_gain.reshape(1, width)
    bias = norm_bias.reshape(1, width)
    partner = [(i, CORES - 1 - i) for i in range(CORES)]
    lists = shortlist.T

    def exchange(x, axis):
        return lax.all_to_all(x, axis, split_axis=0, concat_axis=0, tiled=True)

    (share,) = call(
        share_kernel, [((rows + 2 * mem + chips * width + EXTRA, width), BF16)], [SM] + [VM] * 5
    )(here, queries, enc_keys, enc_values, out_proj, dec_state)
    other = lax.ppermute(share, "core", partner)
    wsend = call(pack_kernel, [((width, tokens), BF16)] * chips, [SM, VM])(here, head_weight)
    win = [wsend[0]]
    for o in range(1, chips):
        win.append(lax.ppermute(wsend[o], "chip", [(i, (i + o) % chips) for i in range(chips)]))
    (m,) = call(
        lambda *refs: slots_kernel(*refs, blocks=blocks, group=group, vocs=vocs), [((slots, rows), BF16)], [VM]
    )(lists)
    (mj,) = call(
        lambda *refs: major_kernel(*refs, blocks=blocks, group=group, vocs=vocs), [((pieces, pairs, rows), BF16)], [VM]
    )(lists)
    (parts,) = call(attend_kernel, [((chips, rows + EXTRA, width), BF16)], [SM, SM] + [VM] * 8)(
        here, source_lengths, queries, enc_keys, enc_values, out_proj, dec_state, gain, bias, other
    )
    parts = exchange(parts, "chip")
    c, extras, outgoing = call(
        lambda *refs: residual_kernel(*refs, total=total),
        [((rows, width), F32), ((chips, EXTRA, width), BF16), ((slots, width), BF16)],
        [VM] * 4,
    )(parts, dec_state, gain, m)
    incoming = exchange(outgoing.reshape(pairs, pieces, width), places)
    picks = lists.shape[0]
    facts = jnp.concatenate(
        [lists, target_slot.reshape(1, rows), target_offset.reshape(1, rows), jnp.zeros((16 - picks - 2, rows), I32)], axis=0
    )
    facts = lax.all_gather(facts, "vocab", axis=0, tiled=False)
    (codes,) = call(
        lambda *refs: code_kernel(*refs, blocks=blocks, group=group, picks=picks),
        [((span, 128), F32)],
        [SM, VM],
        scratch=[pltpu.VMEM((span, rows), F32), pltpu.VMEM((span, rows), F32)],
    )(here, facts)
    lines = 3 * (rows // 128)
    height = -(-(span + span // 128 + 2 * group) // 8) * 8
    (half,) = call(
        lambda *refs: half_kernel(*refs, group=group, lines=lines), [((height, BLK), F32)], [SM] + [VM] * (2 + chips)
    )(here, incoming.reshape(chips, span, width), extras, *win)
    half_in = lax.ppermute(half, "core", partner)
    logits, stats = call(
        lambda *refs: score_kernel(*refs, group=group, total=total),
        [((span, BLK), F32), ((pairs, 128), F32)],
        [VM] * 3,
        scratch=[pltpu.VMEM((span, BLK), F32)],
    )(half, half_in, codes)
    back_stats = exchange(stats.reshape(pairs, 1, 128), places).reshape(pairs, 128)
    totals, loss, back = call(
        total_kernel, [((8, rows), F32), ((1, rows), F32), ((span, 128), F32)], [SM, VM, VM, VM]
    )(here, back_stats, mj, m)
    back_in = exchange(back.reshape(vocs, pieces, 128), "vocab").reshape(span, 128)
    (grads,) = call(
        lambda *refs: delta_kernel(*refs, group=group), [((chips, span, width), BF16)], [SM] + [VM] * (3 + chips)
    )(here, logits, codes, back_in, *win)
    returned = exchange(grads.reshape(pairs, pieces, width), places).reshape(slots, width)
    (sums,) = call(sums_kernel, [((8, rows), F32)], [VM] * 3)(back_stats, mj, totals)
    (grad_state,) = call(
        lambda *refs: final_kernel(*refs, total=total), [((rows, width), F32)], [VM] * 5
    )(returned, m, c, gain, sums)
    return (loss.reshape(rows), grad_state)


def solution(mesh):
    src, vocs = mesh.devices.shape
    finer = Mesh(mesh.devices.reshape(src // CORES, CORES, vocs), ("chip", "core", "vocab"))
    feats = ("chip", "core")
    placed = (
        P("vocab", feats),
        P("vocab", None, feats),
        P("vocab", None, feats),
        P("vocab"),
        P(feats, None),
        P("vocab", feats),
        P(feats),
        P(feats),
        P(feats, "vocab"),
        P("vocab", None),
        P("vocab"),
        P("vocab"),
    )
    return jax.shard_map(
        step,
        mesh=finer,
        in_specs=placed,
        out_specs=(P("vocab"), P("vocab", feats)),
        check_vma=False,
    )
```

```python
import math

import jax
import jax.numpy as jnp
from jax import lax
from jax.experimental import pallas as pl
from jax.experimental.pallas import tpu as pltpu
from jax.sharding import Mesh
from jax.sharding import PartitionSpec as P


HD = 128
BLK = 128
MOST = 2
EPSILON = 1e-05
MASKED = -1e30
F32 = jnp.float32
BF16 = jnp.bfloat16
I32 = jnp.int32

VM = pl.BlockSpec(memory_space=pltpu.VMEM)
SM = pl.BlockSpec(memory_space=pltpu.SMEM)
CORES = 2
STATS = 8
EXTRA = 16


def near(x):
    return pltpu.with_memory_space_constraint(x, pltpu.VMEM)


def call(body, outs, specs, scratch=()):
    return pl.pallas_call(
        body,
        out_shape=tuple(jax.ShapeDtypeStruct(s, d) for s, d in outs),
        in_specs=specs,
        out_specs=tuple(VM for _ in outs),
        scratch_shapes=list(scratch),
    )


def dot(a, b, ca, cb):
    return lax.dot_general(a, b, (((ca,), (cb,)), ((), ())), preferred_element_type=F32)


def thirds(x):
    hi = x.astype(BF16)
    rest = x - hi.astype(F32)
    mid = rest.astype(BF16)
    low = (rest - mid.astype(F32)).astype(BF16)
    return hi, mid, low


def stack_rows(lines, count, width):
    sub = lax.broadcasted_iota(I32, (count, width), 0)
    out = jnp.zeros((count, width), F32)
    for n, line in enumerate(lines):
        out = jnp.where(sub == n, line.astype(F32), out)
    return out


def pack_kernel(where_ref, head_ref, *out_refs):
    chips = len(out_refs)
    _, tokens = out_refs[0].shape
    cols = head_ref.shape[1]
    for o in range(chips):
        to = lax.rem(where_ref[0] + o, chips)
        start = pl.multiple_of(to * tokens, BLK)
        for t in range(tokens // BLK):
            first = start + t * BLK
            there = first < cols
            safe = pl.multiple_of(jnp.minimum(first, cols - BLK), BLK)
            piece = head_ref[:, pl.ds(safe, BLK)]
            out_refs[o][:, t * BLK : (t + 1) * BLK] = jnp.where(there, piece, jnp.zeros_like(piece))


def share_kernel(where_ref, q_ref, k_ref, v_ref, proj_ref, dec_ref, out_ref):
    rows, width = q_ref.shape
    mem = k_ref.shape[1]
    chips = proj_ref.shape[1] // (CORES * width)
    other = 1 - where_ref[1]
    out_ref[0:rows, :] = q_ref[...]
    out_ref[rows : rows + mem, :] = k_ref[0]
    out_ref[rows + mem : rows + 2 * mem, :] = v_ref[0]
    base = rows + 2 * mem
    for y in range(chips):
        cols = pl.ds(pl.multiple_of((y * CORES + other) * width, width), width)
        out_ref[base + y * width : base + (y + 1) * width, :] = proj_ref[:, cols]
    base = base + chips * width
    sums = dot(jnp.ones((8, proj_ref.shape[1]), BF16), proj_ref[...], 1, 1)
    dec_sums = dot(jnp.ones((8, width), BF16), dec_ref[...], 1, 1)
    lines = list(thirds(sums[0:1, :]))
    for third in thirds(dec_sums[0:1, :]):
        lines += [third[:, c * 128 : (c + 1) * 128] for c in range(rows // 128)]
    out_ref[base:, :] = stack_rows(lines, EXTRA, width).astype(BF16)


def mask_of(listed, earlier, u, v, j, blocks, group):
    local = u * group + lax.rem(j, group)
    block = jnp.where(local < blocks, v * blocks + local, -1)
    named = block == listed[0:1, :]
    for k in range(1, listed.shape[0]):
        named = jnp.logical_or(named, block == listed[k : k + 1, :])
    named = named.astype(F32)
    rank = dot(named.astype(BF16), earlier, 1, 0)
    return jnp.where(rank == lax.div(j, group).astype(F32), named, 0.0), block


def earlier_of(rows):
    r0 = lax.broadcasted_iota(I32, (rows, rows), 0)
    r1 = lax.broadcasted_iota(I32, (rows, rows), 1)
    return (r0 < r1).astype(F32).astype(BF16)


def code_kernel(where_ref, list_ref, tslot_ref, toff_ref, code_ref, *, blocks, group):
    pieces = group * MOST
    span = code_ref.shape[0]
    listed = list_ref[...]
    tslot = tslot_ref[...]
    rows = listed.shape[1]
    target_block = jnp.zeros((1, rows), I32)
    for k in range(listed.shape[0]):
        target_block = jnp.where(tslot == k, listed[k : k + 1, :], target_block)
    i = lax.broadcasted_iota(I32, (span, 1), 0)
    u = jnp.full((span, 1), where_ref[0], I32)
    m, block = mask_of(listed, earlier_of(rows), u, lax.div(i, pieces), lax.rem(i, pieces), blocks, group)
    hit = jnp.where(block == target_block, toff_ref[...].astype(F32) + 1.0, 0.0)
    code = jnp.sum(m * (hit + 1.0), axis=1, keepdims=True) - 2.0
    code_ref[...] = jnp.broadcast_to(code, code_ref.shape).astype(BF16)


def block_of(u, v, at, blocks, group):
    local = u * group + at
    return jnp.where(local < blocks, v * blocks + local, -1)


def named_ranks(listed, earlier, block):
    named = block == listed[0:1, :]
    for k in range(1, listed.shape[0]):
        named = jnp.logical_or(named, block == listed[k : k + 1, :])
    named = named.astype(F32)
    rank = dot(named.astype(BF16), earlier, 1, 0)
    return jnp.where(named > 0.0, rank, -1.0)


def slots_kernel(list_ref, m_ref, *, blocks, group, vocs):
    slots, rows = m_ref.shape
    listed = list_ref[...]
    earlier = earlier_of(rows)
    step = 256
    span = vocs * group
    sub = lax.broadcasted_iota(I32, (step, 1), 0)

    def travel(t, carry):
        i = t * step + sub
        v = lax.div(lax.rem(i, span), group)
        block = block_of(lax.div(i, span), v, lax.rem(i, group), blocks, group)
        rank = named_ranks(listed, earlier, block).reshape(step // group, group, rows)
        both = jnp.concatenate([(rank == n).astype(F32) for n in range(MOST)], axis=1)
        size = MOST * step
        m_ref[pl.ds(pl.multiple_of(t * size, size), size), :] = both.reshape(size, rows).astype(BF16)
        return carry

    lax.fori_loop(0, slots // (MOST * step), travel, 0)


def major_kernel(list_ref, mj_ref, *, blocks, group, vocs):
    _, pairs, rows = mj_ref.shape
    listed = list_ref[...]
    earlier = earlier_of(rows)
    w = lax.broadcasted_iota(I32, (pairs, 1), 0)

    def major(t, carry):
        at = jnp.full((pairs, 1), t, I32)
        block = block_of(lax.div(w, vocs), lax.rem(w, vocs), at, blocks, group)
        rank = named_ranks(listed, earlier, block)
        for n in range(MOST):
            mj_ref[n * group + t] = (rank == n).astype(F32).astype(BF16)
        return carry

    lax.fori_loop(0, group, major, 0)


def whole_line(lines, first, n):
    cut = [lines[first + i : first + i + 1] for i in range(3 * n)]
    return jnp.concatenate([cut[c] + cut[n + c] + cut[2 * n + c] for c in range(n)], axis=1)


def attend(q, k, v, length):
    scores = dot(q, k, 1, 1) * (1.0 / math.sqrt(HD))
    usable = lax.broadcasted_iota(I32, scores.shape, 1) < length
    scores = jnp.where(usable, scores, MASKED)
    top = jnp.max(scores, axis=1, keepdims=True)
    raw = jnp.where(usable, jnp.exp(scores - top), 0.0)
    totals = jnp.sum(raw, axis=1, keepdims=True)
    return (dot(raw.astype(BF16), v, 1, 0) / totals).astype(BF16)


def attend_kernel(
    where_ref, len_ref, q_ref, k_ref, v_ref, proj_ref, dec_ref, gain_ref, bias_ref, other_ref, out_ref
):
    chips, _, width = out_ref.shape
    rows = q_ref.shape[0]
    mem = k_ref.shape[1]
    core = where_ref[1]
    length = len_ref[0]
    att = attend(q_ref[...], k_ref[0], v_ref[0], length)
    q2, k2, v2 = other_ref[0:rows, :], other_ref[rows : rows + mem, :], other_ref[rows + mem : rows + 2 * mem, :]
    att2 = attend(q2, k2, v2, length)
    base = rows + 2 * mem
    for y in range(chips):
        own = proj_ref[:, pl.ds(pl.multiple_of((y * CORES + core) * width, width), width)]
        out_ref[y, :rows, :] = (
            dot(att, own, 1, 0) + dot(att2, other_ref[base + y * width : base + (y + 1) * width, :], 1, 0)
        ).astype(BF16)
    base = base + chips * width
    sums = dot(jnp.ones((8, proj_ref.shape[1]), BF16), proj_ref[...], 1, 1)
    part = dot(jnp.ones((8, width), BF16), dec_ref[...], 1, 1)
    for third in thirds(sums):
        part = part + dot(third, att, 1, 1)
    other_sums = dot(other_ref[base:, :], att2, 1, 1)
    line = part[0:1, :] + (other_sums[0:1, :] + other_sums[1:2, :] + other_sums[2:3, :])
    line = line + whole_line(other_ref[base:, :].astype(F32), 3, rows // 128)
    lines = []
    for third in thirds(line):
        lines += [third[:, c * 128 : (c + 1) * 128] for c in range(rows // 128)]
    lines += list(thirds(gain_ref[...])) + list(thirds(bias_ref[...]))
    extra = stack_rows(lines, EXTRA, width).astype(BF16)
    for y in range(chips):
        out_ref[y, rows:, :] = extra


def columns(line):
    n = line.shape[1] // 128
    parts = [jnp.transpose(jnp.broadcast_to(line[:, c * 128 : (c + 1) * 128], (8, 128)))[:, 0:1] for c in range(n)]
    return jnp.concatenate(parts, axis=0)


def residual_kernel(part_ref, dec_ref, gain_ref, m_ref, c_ref, extra_ref, out_ref, *, total):
    chips, _, width = part_ref.shape
    rows = dec_ref.shape[0]
    acc = dec_ref[...].astype(F32)
    lines = jnp.zeros((EXTRA, width), F32)
    for y in range(chips):
        acc = acc + part_ref[y, :rows, :].astype(F32)
        lines = lines + part_ref[y, rows:, :].astype(F32)
        extra_ref[y] = part_ref[y, rows:, :]
    line = whole_line(lines, 0, rows // 128)
    c = acc - columns(line) / total
    c_ref[...] = c
    x = (c * gain_ref[...]).astype(BF16)
    out_ref[...] = dot(m_ref[...], x, 1, 0).astype(BF16)


def third_sum(x, first):
    return x[first : first + 1] + x[first + 1 : first + 2] + x[first + 2 : first + 3]


def half_kernel(where_ref, x_ref, extra_ref, *refs, group, lines):
    w_refs, out_ref = refs[:-1], refs[-1]
    chips, slots, width = x_ref.shape
    tokens = group * BLK
    acc = jnp.zeros((slots, tokens), F32)
    sums = jnp.zeros((EXTRA, tokens), F32)
    squares = jnp.zeros((slots, width), F32)
    for o in range(chips):
        y = lax.rem(where_ref[0] + (chips - o), chips)
        x = x_ref[y]
        w = w_refs[o][...]
        acc = acc + dot(x, w, 1, 0)
        small = extra_ref[y]
        plain = x.astype(F32) / third_sum(small.astype(F32), lines)
        squares = squares + plain * plain
        sums = sums + dot(small, w, 1, 0)
    place = lax.rem(lax.broadcasted_iota(I32, (slots, 1), 0), group)
    dots = acc[:, 0:BLK]
    for b in range(1, group):
        dots = jnp.where(place == b, acc[:, b * BLK : (b + 1) * BLK], dots)
    out_ref[0:slots, :] = dots
    ones = jnp.ones((8, width), BF16)
    total = jnp.zeros((8, slots), F32)
    for third in thirds(squares):
        total = total + dot(ones, third, 1, 1)
    base = slots
    n = slots // 128
    for c in range(n):
        out_ref[base + c : base + c + 1, :] = total[0:1, c * 128 : (c + 1) * 128]
    base = base + n
    for first in (lines, lines + 3):
        line = third_sum(sums, first)
        for b in range(group):
            out_ref[base + b : base + b + 1, :] = line[:, b * BLK : (b + 1) * BLK]
        base = base + group
    if base < out_ref.shape[0]:
        out_ref[base:, :] = jnp.zeros((out_ref.shape[0] - base, BLK), F32)


def score_kernel(own_ref, other_ref, code_ref, l_ref, row_ref, stat_ref, *, group, total):
    slots = l_ref.shape[0]
    pieces = MOST * group
    both = own_ref[...] + other_ref[...]
    dots = both[0:slots]
    n = slots // 128
    squares = columns(jnp.concatenate([both[slots + c : slots + c + 1] for c in range(n)], axis=1))
    inv = lax.rsqrt(squares / total + EPSILON)
    place = lax.rem(lax.broadcasted_iota(I32, (slots, 1), 0), group)
    at = slots + n
    gains = jnp.broadcast_to(both[at : at + 1], dots.shape)
    biases = jnp.broadcast_to(both[at + group : at + group + 1], dots.shape)
    for b in range(1, group):
        gains = jnp.where(place == b, both[at + b : at + b + 1], gains)
        biases = jnp.where(place == b, both[at + group + b : at + group + b + 1], biases)
    bare = inv * dots
    logits = bare + biases
    l_ref[...] = logits
    top = jnp.max(logits, axis=1, keepdims=True)
    shifted = jnp.exp(logits - top)
    spread = jnp.sum(shifted, axis=1, keepdims=True)
    lse = top + jnp.log(spread)
    soft = shifted / spread
    lane = lax.broadcasted_iota(I32, logits.shape, 1)
    hit = lane.astype(F32) == code_ref[...].astype(F32)

    def row_sum(v):
        return jnp.sum(v, axis=1, keepdims=True)

    cols = [
        lse,
        row_sum(jnp.where(hit, logits, 0.0)),
        inv,
        row_sum(soft * gains),
        row_sum(soft * bare),
        row_sum(jnp.where(hit, gains, 0.0)),
        row_sum(jnp.where(hit, bare, 0.0)),
    ]
    out = jnp.zeros(logits.shape, F32)
    for n, col in enumerate(cols):
        out = jnp.where(lane == n, col, out)
    stat_ref[...] = out
    sents = slots // pieces
    lane_s = lax.div(lax.broadcasted_iota(I32, (sents, 128), 1), STATS)
    packed = jnp.zeros((sents, 128), F32)
    for j in range(pieces):
        z = stat_ref[pl.ds(j, sents, stride=pieces), :]
        if j:
            z = pltpu.roll(z, j * STATS, 1)
        packed = jnp.where(lane_s == j, z, packed)
    for u in range(row_ref.shape[0] // sents):
        row_ref[u * sents : (u + 1) * sents, :] = packed


def total_kernel(where_ref, e_ref, mj_ref, m_ref, tot_ref, loss_ref, back_ref):
    pieces, pairs, rows = mj_ref.shape
    low = jnp.full((8, rows), MASKED, F32)
    for j in range(pieces):
        lse = jnp.where(mj_ref[j].astype(F32) > 0.0, e_ref[:, j * STATS : j * STATS + 1], MASKED)
        low = jnp.maximum(low, jnp.max(lse.reshape(pairs // 8, 8, rows), axis=0))
    low = jnp.max(low, axis=0, keepdims=True)
    total = jnp.zeros((8, rows), F32)
    picked = jnp.zeros((8, rows), F32)
    for j in range(pieces):
        there = mj_ref[j].astype(F32) > 0.0
        lse = e_ref[:, j * STATS : j * STATS + 1]
        pick = e_ref[:, j * STATS + 1 : j * STATS + 2]
        total = total + jnp.sum(jnp.where(there, jnp.exp(lse - low), 0.0).reshape(pairs // 8, 8, rows), axis=0)
        picked = picked + jnp.sum(jnp.where(there, pick, 0.0).reshape(pairs // 8, 8, rows), axis=0)
    log_total = low + jnp.log(jnp.sum(total, axis=0, keepdims=True))
    tot_ref[...] = jnp.broadcast_to(log_total, tot_ref.shape)
    loss_ref[...] = log_total - jnp.sum(picked, axis=0, keepdims=True)
    slots = back_ref.shape[0]
    own = m_ref[pl.ds(pl.multiple_of(where_ref[0] * slots, slots), slots), :].astype(F32)
    back_ref[...] = jnp.broadcast_to(jnp.sum(own * log_total, axis=1, keepdims=True), back_ref.shape)


def delta_kernel(where_ref, l_ref, code_ref, back_ref, *refs, group):
    w_refs, out_ref = refs[:-1], refs[-1]
    chips = len(w_refs)
    logits = l_ref[...]
    code = code_ref[...].astype(F32)
    lane = lax.broadcasted_iota(I32, logits.shape, 1).astype(F32)
    deltas = jnp.exp(logits - back_ref[...]) - jnp.where(lane == code, 1.0, 0.0)
    deltas = jnp.where(code > -1.5, deltas, 0.0)
    place = lax.rem(lax.broadcasted_iota(I32, logits.shape, 0), group)
    wide = jnp.concatenate([jnp.where(place == b, deltas, 0.0).astype(BF16) for b in range(group)], axis=1)
    for o in range(chips):
        y = lax.rem(where_ref[0] + (chips - o), chips)
        out_ref[y] = dot(wide, w_refs[o][...], 1, 1).astype(BF16)


def sums_kernel(e_ref, mj_ref, tot_ref, out_ref):
    pieces, pairs, rows = mj_ref.shape
    log_total = tot_ref[0:1, :]
    sum_g = jnp.zeros((8, rows), F32)
    sum_gx = jnp.zeros((8, rows), F32)
    inv = jnp.zeros((8, rows), F32)
    for j in range(pieces):
        there = mj_ref[j].astype(F32) > 0.0

        def col(n):
            return e_ref[:, j * STATS + n : j * STATS + n + 1]

        share = jnp.exp(col(0) - log_total)
        g = jnp.where(there, share * col(3) - col(5), 0.0).reshape(pairs // 8, 8, rows)
        gx = jnp.where(there, share * col(4) - col(6), 0.0).reshape(pairs // 8, 8, rows)
        sum_g = sum_g + jnp.sum(g, axis=0)
        sum_gx = sum_gx + jnp.sum(gx, axis=0)
        inv = jnp.maximum(inv, jnp.max(jnp.where(there, col(2), 0.0).reshape(pairs // 8, 8, rows), axis=0))
    sub = lax.broadcasted_iota(I32, (8, rows), 0)
    sum_g = jnp.sum(sum_g, axis=0, keepdims=True)
    sum_gx = jnp.sum(sum_gx, axis=0, keepdims=True)
    inv = jnp.max(inv, axis=0, keepdims=True)
    out_ref[...] = jnp.where(sub == 0, sum_g, jnp.where(sub == 1, sum_gx, inv))


def final_kernel(r_ref, m_ref, c_ref, gain_ref, sums_ref, out_ref, *, total):
    grad = dot(m_ref[...], r_ref[...], 0, 0)
    rows = grad.shape[0]
    cols = jnp.concatenate(
        [jnp.transpose(sums_ref[:, c * 128 : (c + 1) * 128])[:, 0:3] for c in range(rows // 128)], axis=0
    )
    inv = cols[:, 2:3]
    g = grad * gain_ref[...]
    centered = c_ref[...] * inv
    out_ref[...] = inv * (g - cols[:, 0:1] / total - centered * (cols[:, 1:2] / total))


def step(
    queries,
    enc_keys,
    enc_values,
    source_lengths,
    out_proj,
    dec_state,
    norm_gain,
    norm_bias,
    head_weight,
    shortlist,
    target_slot,
    target_offset,
):
    vocs = lax.axis_size("vocab")
    chips = lax.axis_size("chip")
    places = ("chip", "vocab")
    rows, width = dec_state.shape
    mem = enc_keys.shape[1]
    total = out_proj.shape[1]
    blocks = head_weight.shape[1] // BLK
    group = -(-blocks // chips)
    tokens = group * BLK
    pieces = group * MOST
    pairs = chips * vocs
    slots = pairs * pieces
    span = vocs * pieces
    here = jnp.stack([lax.axis_index("chip"), lax.axis_index("core"), lax.axis_index("vocab")]).astype(I32)
    gain = norm_gain.reshape(1, width)
    bias = norm_bias.reshape(1, width)
    partner = [(i, CORES - 1 - i) for i in range(CORES)]
    lists = shortlist.T

    def exchange(x, axis):
        return lax.all_to_all(x, axis, split_axis=0, concat_axis=0, tiled=True)

    (share,) = call(
        share_kernel, [((rows + 2 * mem + chips * width + EXTRA, width), BF16)], [SM] + [VM] * 5
    )(here, queries, enc_keys, enc_values, out_proj, dec_state)
    other = lax.ppermute(share, "core", partner)
    wsend = call(pack_kernel, [((width, tokens), BF16)] * chips, [SM, VM])(here, head_weight)
    win = [wsend[0]]
    for o in range(1, chips):
        win.append(lax.ppermute(wsend[o], "chip", [(i, (i + o) % chips) for i in range(chips)]))
    (m,) = call(
        lambda *refs: slots_kernel(*refs, blocks=blocks, group=group, vocs=vocs), [((slots, rows), BF16)], [VM]
    )(lists)
    (mj,) = call(
        lambda *refs: major_kernel(*refs, blocks=blocks, group=group, vocs=vocs), [((pieces, pairs, rows), BF16)], [VM]
    )(lists)
    (parts,) = call(attend_kernel, [((chips, rows + EXTRA, width), BF16)], [SM, SM] + [VM] * 8)(
        here, source_lengths, queries, enc_keys, enc_values, out_proj, dec_state, gain, bias, near(other)
    )
    parts = exchange(parts, "chip")
    c, extras, outgoing = call(
        lambda *refs: residual_kernel(*refs, total=total),
        [((rows, width), F32), ((chips, EXTRA, width), BF16), ((slots, width), BF16)],
        [VM] * 4,
    )(near(parts), dec_state, gain, m)
    incoming = exchange(outgoing.reshape(pairs, pieces, width), places)
    (code,) = call(
        lambda *refs: code_kernel(*refs, blocks=blocks, group=group), [((span, 128), BF16)], [SM, VM, VM, VM]
    )(here, lists, target_slot.reshape(1, rows), target_offset.reshape(1, rows))
    codes = exchange(code.reshape(vocs, pieces, 128), "vocab").reshape(span, 128)
    lines = 3 * (rows // 128)
    height = -(-(span + span // 128 + 2 * group) // 8) * 8
    (half,) = call(
        lambda *refs: half_kernel(*refs, group=group, lines=lines), [((height, BLK), F32)], [SM] + [VM] * (2 + chips)
    )(here, near(incoming.reshape(chips, span, width)), extras, *win)
    half_in = lax.ppermute(half, "core", partner)
    logits, stats = call(
        lambda *refs: score_kernel(*refs, group=group, total=total),
        [((span, BLK), F32), ((pairs, 128), F32)],
        [VM] * 3,
        scratch=[pltpu.VMEM((span, BLK), F32)],
    )(half, near(half_in), codes)
    back_stats = exchange(stats.reshape(pairs, 1, 128), places).reshape(pairs, 128)
    totals, loss, back = call(
        total_kernel, [((8, rows), F32), ((1, rows), F32), ((span, 128), F32)], [SM, VM, VM, VM]
    )(here, near(back_stats), mj, m)
    back_in = exchange(back.reshape(vocs, pieces, 128), "vocab").reshape(span, 128)
    (grads,) = call(
        lambda *refs: delta_kernel(*refs, group=group), [((chips, span, width), BF16)], [SM] + [VM] * (3 + chips)
    )(here, logits, codes, near(back_in), *win)
    returned = exchange(grads.reshape(pairs, pieces, width), places).reshape(slots, width)
    (sums,) = call(sums_kernel, [((8, rows), F32)], [VM] * 3)(back_stats, mj, totals)
    (grad_state,) = call(
        lambda *refs: final_kernel(*refs, total=total), [((rows, width), F32)], [VM] * 5
    )(near(returned), m, c, gain, sums)
    return (loss.reshape(rows), grad_state)


def solution(mesh):
    src, vocs = mesh.devices.shape
    finer = Mesh(mesh.devices.reshape(src // CORES, CORES, vocs), ("chip", "core", "vocab"))
    feats = ("chip", "core")
    placed = (
        P("vocab", feats),
        P("vocab", None, feats),
        P("vocab", None, feats),
        P("vocab"),
        P(feats, None),
        P("vocab", feats),
        P(feats),
        P(feats),
        P(feats, "vocab"),
        P("vocab", None),
        P("vocab"),
        P("vocab"),
    )
    return jax.shard_map(
        step,
        mesh=finer,
        in_specs=placed,
        out_specs=(P("vocab"), P("vocab", feats)),
        check_vma=False,
    )
```
